128 devices in a mesh: dp: 32 (over z, y, core), tm: 4 (over x).
Axes of the slice: x: 4, y: 4, z: 4, core: 2. Of those that a mesh axis runs over, the one named last changes fastest.
Arguments:
- student: bfloat16 [256, 1024, 128], P(('dp', 'tm')), may hold values from -6 to 6
- teacher: bfloat16 [256, 1024, 128], P(('dp', 'tm')), may hold values from -200 to 200
- partner_dp: int32 [256, 8], replicated, may hold values from 0 to 31, all different within a row; in each aligned block of 2 rows (0 to 1, 2 to 3, ...) no two rows name the same one
- partner_slot: int32 [256, 8], replicated, may hold values from 0 to 1
- valid_frames: int32 [256], replicated, may hold values from 256 to 1024, as said below
Outputs:
- loss: float32 [], replicated
- grad_student: bfloat16 [256, 1024, 128], P(('dp', 'tm'))
The draws below stay inside these ranges and needn't reach their ends.
Inputs may be any that keep to these rules, and one draw needn't show every extreme that they name: `partner_dp`: among the partner entries of the 2 blocks of one device no dp index appears more than 1 times; the 8 entries of one block are distinct. A partner may be the block itself. `valid_frames`: block 0 is full and block 1 has the fewest valid frames.
All inputs are finite; a program needn't handle non-finite values.
Results may differ from the reference program's by a relative error of at most 0.0042.
Values may be sent and summed in bfloat16 or wider, within the bound.
A program may use at most 64 MiB of HBM per device.

```python
import math
import jax
import jax.numpy as jnp
import numpy as np
from jax import lax

E = 128
BLK = 1024
K = 8
BLK_DEV = 2
NB = 256
MOST = 1
N_DP = 32
N_TM = 4


def shared_student(key):
    return jnp.clip(jax.random.normal(jax.random.fold_in(key, 11), (NB, BLK, E), jnp.float32), -6.0, 6.0)


def draw_student(key, part):
    return shared_student(key).astype(jnp.bfloat16)


def draw_teacher(key, part):
    teacher_key = jax.random.fold_in(key, 23)
    values = jax.random.normal(teacher_key, (NB, BLK, E), jnp.float32)
    return jnp.clip(values, -200.0, 200.0).astype(jnp.bfloat16)


def draw_valid_frames(key, part):
    lengths = jax.random.randint(jax.random.fold_in(key, 37), (NB,), BLK // 4, BLK + 1, dtype=jnp.int32)
    return lengths.at[0].set(BLK).at[1].set(BLK // 4)


def plant(entries, rng, low, top_value):
    place = [jax.random.randint(jax.random.fold_in(rng, axis), (), 0, length) for axis, length in enumerate(entries.shape)]
    widest = entries.shape.index(max(entries.shape))
    next_to = place[:widest] + [(place[widest] + 1) % entries.shape[widest]] + place[widest + 1:]
    return entries.at[tuple(place)].set(low).at[tuple(next_to)].set(top_value)


def shared_out(key, own, number, rows, amount, top, bound, lean):
    sequence = jax.random.permutation(key, amount)
    crowded, ordinary = portions_of(amount, rows * top, bound, lean, True), portions_of(amount, rows * top, bound, lean, False)
    places = jnp.arange(amount)

    def named(sizes, turn):
        used = int((sizes > 0).sum())
        fixed = max(1, used // 4)
        shifted = fixed + (places - fixed + turn * (used - fixed)) % max(1, amount - fixed)
        return jnp.zeros((amount,), jnp.int32).at[sequence[jnp.where(places < fixed, places, shifted)]].set(jnp.asarray(sizes, jnp.int32))

    sizes = jnp.where(number % 4 == 0, named(crowded, number // 4), named(ordinary, number - number // 4 - 1))
    mixed = jax.random.permutation(jax.random.fold_in(own, 3), amount)
    giver, receiver = mixed[0:amount // 2 * 2:2], mixed[1:amount // 2 * 2:2]
    margin = jnp.minimum(sizes[giver] - 1, bound - sizes[receiver]) // 2
    margin = jnp.where((giver == sequence[0]) | (receiver == sequence[0]) | (sizes[receiver] == 0), 0, jnp.maximum(margin, 0))
    shifted = jax.random.randint(jax.random.fold_in(own, 4), (amount // 2,), 0, 1 << 20) % (margin + 1)
    sizes = sizes.at[giver].add(-shifted).at[receiver].add(shifted)
    labels = jnp.searchsorted(jnp.cumsum(sizes), jnp.arange(rows * top), side="right").astype(jnp.int32)
    table = labels.reshape(top, rows).T
    table = table[jax.random.permutation(jax.random.fold_in(own, 1), rows)]
    turn = jax.random.randint(jax.random.fold_in(own, 2), (rows, 1), 0, top)
    return jnp.take_along_axis(table, (jnp.arange(top)[None, :] + turn) % top, axis=1)


def portions_of(count, total, bound, slope, full):
    portions = [(1 << 20) // math.isqrt(grade ** slope) + 1 for grade in range(1, count + 1)]
    largest = bound if full else min(bound, max(-(-total // count), total * portions[0] // sum(portions)))
    least = 1 if total - largest >= count - 1 else 0
    given, rest = [largest] + [least] * (count - 1), total - largest - least * (count - 1)
    while rest > 0:
        candidates = [i for i in range(1, count) if given[i] < largest] or [i for i in range(1, count) if given[i] < bound]
        pool, remaining = sum([portions[i] for i in candidates]), rest
        for i in candidates:
            addition = min(bound - given[i], max(1, remaining * portions[i] // pool), rest)
            given[i] = given[i] + addition
            rest = rest - addition
    return np.array(given)


def setup_inputs(seed: int = 0) -> dict:
    key_of = jax.random.split(jax.random.key(seed), 6)
    student = draw_student(jax.random.fold_in(key_of[5], 71), 0)
    teacher = draw_teacher(jax.random.fold_in(key_of[5], 71), 0)
    partner_dp_keys = jax.random.split(jax.random.fold_in(key_of[2], 1), NB // BLK_DEV)
    partner_dp_turns = jax.random.permutation(jax.random.fold_in(key_of[2], 3), NB // BLK_DEV)
    partner_dp = jax.vmap(lambda own, number: shared_out(jax.random.fold_in(key_of[2], 2), own, number, BLK_DEV, N_DP, K, MOST, 2))(partner_dp_keys, partner_dp_turns).reshape((NB, K))
    partner_slot = plant(jax.random.randint(key_of[3], (NB, K), 0, BLK_DEV), jax.random.fold_in(key_of[3], 1), 0, BLK_DEV - 1).astype(jnp.int32)
    valid_frames = draw_valid_frames(jax.random.fold_in(key_of[5], 71), 0)
    return dict(student=student, teacher=teacher, partner_dp=partner_dp, partner_slot=partner_slot, valid_frames=valid_frames)


NEG_FILL = -1e+30

def reference(student, teacher, partner_dp, partner_slot, valid_frames):
    blocks = student.shape[0]
    block_ids = jnp.arange(blocks, dtype=jnp.int32)
    time_slot = block_ids // BLK_DEV % N_TM
    partners = (partner_dp * N_TM + time_slot[:, None]) * BLK_DEV + partner_slot
    tile_ids = jnp.concatenate([block_ids[:, None], partners], axis=1).astype(jnp.int32)
    frame_ids = jnp.arange(BLK, dtype=jnp.int32)
    score_scale = 1.0 / math.sqrt(E)
    positive = lax.optimization_barrier(jnp.sum(student.astype(jnp.float32) * teacher.astype(jnp.float32), axis=2)) * score_scale
    query_all = frame_ids[None, :] < valid_frames[:, None]
    first_tile = (jnp.arange(K + 1) == 0)[:, None, None]
    diagonal = frame_ids[:, None] == frame_ids[None, :]

    def tile_scores(block):
        key_rows = teacher[tile_ids[block]].astype(jnp.float32)
        query_rows = student[block].astype(jnp.float32)
        scores = jnp.einsum('ie,kje->kij', query_rows, key_rows) * score_scale
        key_ok = frame_ids[None, :] < valid_frames[tile_ids[block]][:, None]
        query_ok = frame_ids < valid_frames[block]
        return (scores, key_rows, key_ok, query_ok)

    def forward(block):
        scores, key_rows, key_ok, query_ok = tile_scores(block)
        row_masked = jnp.where(key_ok[:, None, :], scores, NEG_FILL)
        row_best = lax.optimization_barrier(jnp.max(row_masked, axis=(0, 2)))
        row_sum = lax.optimization_barrier(jnp.sum(jnp.exp(row_masked - row_best[None, :, None]), axis=(0, 2)))
        col_masked = jnp.where(query_ok[None, :, None], scores, NEG_FILL)
        col_best = lax.optimization_barrier(jnp.max(col_masked, axis=1))
        col_sum = lax.optimization_barrier(jnp.sum(jnp.exp(col_masked - col_best[:, None, :]), axis=1))
        return (row_best + jnp.log(row_sum), col_best, col_sum)
    row_lse, col_best, col_sum = lax.map(forward, block_ids)
    targets = tile_ids.reshape(-1)
    flat_best = col_best.reshape(-1, BLK)
    flat_sum = col_sum.reshape(-1, BLK)
    best = jax.ops.segment_max(flat_best, targets, num_segments=blocks)
    summed = jax.ops.segment_sum(flat_sum * jnp.exp(flat_best - best[targets]), targets, num_segments=blocks)
    col_lse = best + jnp.log(jnp.where(query_all, summed, 1.0))
    row_terms = jnp.sum(jnp.where(query_all, row_lse - positive, 0.0))
    col_terms = jnp.sum(jnp.where(query_all, col_lse - positive, 0.0))
    loss = 0.5 * (row_terms + col_terms) / jnp.sum(valid_frames).astype(jnp.float32)

    def backward(block):
        scores, key_rows, key_ok, query_ok = tile_scores(block)
        pair_ok = query_ok[None, :, None] & key_ok[:, None, :]
        prob_row = jnp.exp(scores - row_lse[block][None, :, None])
        prob_col = jnp.exp(scores - col_lse[tile_ids[block]][:, None, :])
        grad_scores = jnp.where(pair_ok, 0.5 * (prob_row + prob_col), 0.0)
        grad_scores = grad_scores - jnp.where(first_tile & diagonal[None] & query_ok[None, :, None], 1.0, 0.0)
        grad_low = lax.optimization_barrier(grad_scores.astype(jnp.bfloat16)).astype(jnp.float32)
        return (jnp.einsum('kij,kje->ie', grad_low, key_rows) * score_scale).astype(jnp.bfloat16)
    grad_student = lax.map(backward, block_ids)
    return (loss, grad_student)
```

```python
import functools
import heapq
import math

import jax
import jax.numpy as jnp
from jax import lax
from jax.experimental import pallas as pl
from jax.experimental.pallas import tpu as pltpu
from jax.sharding import PartitionSpec as P

MESH = pl.DeviceIdType.MESH
F32 = jnp.float32
BIG = 1e30

ZP, ZM, YP, YM = range(4)
MOVE = {ZP: (1, 0), ZM: (-1, 0), YP: (0, 1), YM: (0, -1)}


PARTS = 2


def onward(tile, oz, oy, part):
    half = part * 2 // PARTS
    first, second = (oz, oy) if tile == 0 else (oy, oz)
    plus1, minus1 = (ZP, ZM) if tile == 0 else (YP, YM)
    plus2, minus2 = (YP, YM) if tile == 0 else (ZP, ZM)
    links = []
    if second == 0:
        if first == 0:
            links += [plus1, minus1]
        elif first == 1 and half == 0:
            links += [plus1]
        elif first == 3 and half == 1:
            links += [minus1]
        links += [plus2, minus2]
    elif second == 1 and half == 0:
        links += [plus2]
    elif second == 3 and half == 1:
        links += [minus2]
    return links


def moved(oz, oy, link):
    dz, dy = MOVE[link]
    return (oz + dz) % 4, (oy + dy) % 4


def plan():
    free = [0.0] * 4
    events, order, count = [], [], 0

    def send(unit, link, now):
        nonlocal count
        tile, oz, oy, half = unit
        start = max(now, free[link])
        free[link] = start + 1.0
        noz, noy = moved(oz, oy, link)
        heapq.heappush(events, (free[link] + 0.5, count, (tile, noz, noy, half), link))
        count += 1

    first = []
    for link in range(4):
        near = 0 if link in (ZP, ZM) else 1
        lead = 0 if link in (ZP, YP) else 1
        for tile in (near, 1 - near):
            for part in range(PARTS):
                first.append(((tile, 0, 0, part if lead == 0 else PARTS - 1 - part), link))
    first = [first[k * 2 * PARTS + i] for i in range(2 * PARTS) for k in range(4)]
    for unit, link in first:
        send(unit, link, 0.0)
    while events:
        now, _, unit, _ = heapq.heappop(events)
        out = onward(*unit)
        order.append((unit, out))
        for link in out:
            send(unit, link, now)
    return first, order, max(free)


def gather_kernel(rows, t_ref, out_ref, send_sem, recv_sem, peer_send, peer_recv, own_sem):
    half_rows = rows // PARTS
    me, tm = lax.axis_index("dp"), lax.axis_index("tm")
    z, y, c = me // 8, (me // 2) % 4, me % 2

    def dp_of(zz, yy, cc):
        return (zz * 4 + yy) * 2 + cc

    near = [
        dp_of((z + 1) % 4, y, c), dp_of((z + 3) % 4, y, c),
        dp_of(z, (y + 1) % 4, c), dp_of(z, (y + 3) % 4, c),
    ]
    peer = dp_of(z, y, 1 - c)
    barrier = pltpu.get_barrier_semaphore()
    for other in near + [peer]:
        pl.semaphore_signal(barrier, inc=1, device_id=(other, tm), device_id_type=MESH)
    pl.semaphore_wait(barrier, 5)

    first, order, _ = plan()
    sends = []

    def recv_id(unit):
        tile, oz, oy, half = unit
        return ((tile * 4 + oz) * 4 + oy) * PARTS + half

    def slot(unit):
        _, oz, oy, _ = unit
        return dp_of((z + 4 - oz) % 4, (y + 4 - oy) % 4, c)

    def place(ref, unit):
        tile, oz, oy, half = unit
        return ref.at[slot(unit), tile, pl.ds(half * half_rows, half_rows)]

    def source(unit):
        tile, oz, oy, half = unit
        if oz == 0 and oy == 0:
            return t_ref.at[tile, pl.ds(half * half_rows, half_rows)]
        return place(out_ref, unit)

    def send(unit, link):
        tile, oz, oy, half = unit
        copy = pltpu.make_async_remote_copy(
            src_ref=source(unit), dst_ref=place(out_ref, unit),
            send_sem=send_sem.at[len(sends)], recv_sem=recv_sem.at[recv_id((tile, *moved(oz, oy, link), half))],
            device_id=(near[link], tm), device_id_type=MESH,
        )
        copy.start()
        sends.append(copy)

    shares = []

    def share(unit):
        copy = pltpu.make_async_remote_copy(
            src_ref=source(unit), dst_ref=place(out_ref, unit),
            send_sem=peer_send.at[recv_id(unit)], recv_sem=peer_recv.at[recv_id(unit)],
            device_id=(peer, tm), device_id_type=MESH,
        )
        copy.start()
        shares.append(copy)

    for unit, link in first:
        send(unit, link)
    for tile in (0, 1):
        for half in range(PARTS):
            share((tile, 0, 0, half))
    own = pltpu.make_async_copy(t_ref, out_ref.at[me], own_sem)
    own.start()
    for unit, out in order:
        here = place(out_ref, unit)
        pltpu.make_async_remote_copy(
            src_ref=here, dst_ref=here, send_sem=send_sem.at[0], recv_sem=recv_sem.at[recv_id(unit)],
            device_id=(near[0], tm), device_id_type=MESH,
        ).wait_recv()
        for link in out:
            send(unit, link)
        share(unit)
    for copy in shares:
        copy.wait_send()
        copy.wait_recv()
    for copy in sends:
        copy.wait_send()
    own.wait()


def gather(teacher, dp=32):
    blocks, rows, width = teacher.shape
    first, order, _ = plan()
    n_sends = len(first) + sum(len(o) for _, o in order)
    return pl.pallas_call(
        functools.partial(gather_kernel, rows),
        out_shape=jax.ShapeDtypeStruct((dp, blocks, rows, width), teacher.dtype),
        in_specs=[pl.BlockSpec(memory_space=pltpu.VMEM)],
        out_specs=pl.BlockSpec(memory_space=pl.ANY),
        scratch_shapes=[
            pltpu.SemaphoreType.DMA((n_sends,)), pltpu.SemaphoreType.DMA((32 * PARTS,)),
            pltpu.SemaphoreType.DMA((32 * PARTS,)), pltpu.SemaphoreType.DMA((32 * PARTS,)), pltpu.SemaphoreType.DMA,
        ],
        compiler_params=pltpu.CompilerParams(collective_id=0, has_side_effects=True),
        name="gather",
    )(teacher)


LOW, HIGH = 2.0 ** -60, 2.0 ** 100
STEP = 256


def augment(ref, index, count, key):
    rows, width = ref.shape[-2], 128
    row = lax.broadcasted_iota(jnp.int32, (rows, width), 0)
    lane = lax.broadcasted_iota(jnp.int32, (rows, width), 1)
    mask = jnp.where(row < count, 0.0, -BIG)
    mine, other = (0, 1) if key else (1, 0)
    ref[index, :, width:] = jnp.where(lane == mine, mask, jnp.where(lane == other, 1.0, 0.0)).astype(ref.dtype)


def nt(a, b):
    return lax.dot_general(a, b, (((1,), (1,)), ((), ())), preferred_element_type=F32)


def fetch(meta, every, t_buf, sems, e):
    return pltpu.make_async_copy(every.at[meta[e]], t_buf.at[e, :, pl.ds(0, 128)], sems.at[e])


def first_kernel(tiles, step, meta, s_ref, every, row_ref, send_ref, own_ref, ok_ref, sum_ref,
                 t_buf, s_buf, acc, col, sems):
    frames, width = s_ref.shape[1], s_ref.shape[2]
    total = 2 * tiles
    c2 = 1.0 / math.sqrt(width) / math.log(2.0)
    scale = 1.0 / math.sqrt(width)
    for e in range(total):
        fetch(meta, every, t_buf, sems, e).start()
    for a in range(2):
        s_buf[a, :, :width] = s_ref[a]
        augment(s_buf, a, meta[3 * total + a], False)
    acc[...] = jnp.zeros_like(acc)
    ok_ref[0] = 1
    sum_ref[...] = jnp.zeros_like(sum_ref)
    lane = lax.broadcasted_iota(jnp.int32, (1, frames), 1)
    send_ref[...] = jnp.zeros_like(send_ref)

    def put(e, values):
        a, k = e // tiles, e % tiles

        @pl.when(k == 0)
        def _():
            for r in range(8):
                own_ref[a, r:r + 1, :] = values[:, r * 128:(r + 1) * 128]

        @pl.when(k != 0)
        def _():
            for r in range(8):
                send_ref[meta[2 * total + e], r:r + 1, :] = values[:, r * 128:(r + 1) * 128]

    def tile(e, carry):
        a = e // tiles
        keys = meta[total + e]
        fetch(meta, every, t_buf, sems, e).wait()
        augment(t_buf, e, keys, True)
        col[...] = jnp.zeros_like(col)
        chunks = (meta[3 * total + a] + step - 1) // step
        spans = (keys + STEP - 1) // STEP
        for v in range(1, frames // STEP + 1):
            @pl.when(spans == v)
            def _():
                def chunk(i, c):
                    rows = pl.ds(pl.multiple_of(i * step, step), step)
                    lhs = s_buf[a, rows, :]
                    part = acc[a, rows, :]
                    for j in range(v):
                        cols = slice(j * STEP, (j + 1) * STEP)
                        p = jnp.exp2(nt(lhs, t_buf[e, cols, :]) * c2)
                        for u in range(STEP // 128):
                            part = part + p[:, u * 128:(u + 1) * 128]
                        col[:, cols] += jnp.sum(p.reshape(step // 8, 8, STEP), axis=0)
                    acc[a, rows, :] = part
                    return c
                lax.fori_loop(0, chunks, chunk, 0)
        sums = jnp.sum(col[...], axis=0, keepdims=True)
        real = lane < keys
        low = jnp.min(jnp.where(real, sums, 1.0))
        high = jnp.max(jnp.where(real, sums, 1.0))

        @pl.when(jnp.logical_not((low >= LOW) & (high <= HIGH)))
        def _():
            ok_ref[0] = 0
        put(e, jnp.where(real, jnp.log(jnp.where(real, sums, 1.0)), -BIG))
        return carry

    lax.fori_loop(0, total, tile, 0)

    for a in range(2):
        count = meta[3 * total + a]
        row = lax.broadcasted_iota(jnp.int32, (frames, 128), 0)
        sums = jnp.broadcast_to(jnp.sum(acc[a], axis=1, keepdims=True), (frames, 128))
        sums = jnp.where(row < count, sums, 1.0)

        @pl.when(jnp.logical_not((jnp.min(sums) >= LOW) & (jnp.max(sums) <= HIGH)))
        def _():
            ok_ref[0] = 0
        row_ref[a] = jnp.log(sums)

    @pl.when(ok_ref[0] == 0)
    def _():
        row_ref[...] = jnp.full(row_ref.shape, -BIG, F32)
        acc[...] = jnp.zeros_like(acc)
        half = 128

        def slow_tile(e, carry):
            a = e // tiles
            col[0:1, :] = jnp.full((1, frames), -BIG, F32)
            col[1:2, :] = jnp.zeros((1, frames), F32)

            def slow_chunk(i, c):
                rows = pl.ds(pl.multiple_of(i * half, half), half)
                lhs = s_buf[a, rows, :]
                for j in range(frames // half):
                    cols = slice(j * half, (j + 1) * half)
                    sc = nt(lhs, t_buf[e, cols, :]) * scale
                    old = row_ref[a, rows, :]
                    new = jnp.maximum(old, jnp.broadcast_to(jnp.max(sc, axis=1, keepdims=True), (half, 128)))
                    acc[a, rows, :] = acc[a, rows, :] * jnp.exp(old - new) + jnp.broadcast_to(
                        jnp.sum(jnp.where(sc > -0.01 * BIG, jnp.exp(sc - new[:, :1]), 0.0), axis=1, keepdims=True), (half, 128))
                    row_ref[a, rows, :] = new
                    cold = col[0:1, cols]
                    cnew = jnp.maximum(cold, jnp.max(sc, axis=0, keepdims=True))
                    col[1:2, cols] = col[1:2, cols] * jnp.exp(cold - cnew) + jnp.sum(
                        jnp.where(sc > -0.01 * BIG, jnp.exp(sc - cnew), 0.0), axis=0, keepdims=True)
                    col[0:1, cols] = cnew
                return c
            lax.fori_loop(0, frames // half, slow_chunk, 0)
            real = lane < meta[total + e]
            put(e, jnp.where(real, col[0:1, :] + jnp.log(jnp.where(real, col[1:2, :], 1.0)), -BIG))
            return carry
        lax.fori_loop(0, total, slow_tile, 0)
        for a in range(2):
            row = lax.broadcasted_iota(jnp.int32, (frames, 128), 0)
            row_ref[a] = jnp.where(row < meta[3 * total + a], row_ref[a] + jnp.log(jnp.maximum(acc[a], 1e-30)), 0.0)

    for a in range(2):
        row = lax.broadcasted_iota(jnp.int32, (frames, 128), 0)
        pos = s_ref[a].astype(F32) * t_buf[a * tiles, :, :width].astype(F32)
        terms = jnp.where(row < meta[3 * total + a], row_ref[a] * (1.0 / 128) - (2.0 * scale) * pos, 0.0)
        sum_ref[...] += jnp.sum(terms.reshape(frames // 8, 8, 128), axis=0)


def first_pass(meta, student, every, n_dp, tiles, step=512):
    blocks, frames, width = student.shape
    total = blocks * tiles
    smem, vmem = pl.BlockSpec(memory_space=pltpu.SMEM), pl.BlockSpec(memory_space=pltpu.VMEM)
    return pl.pallas_call(
        functools.partial(first_kernel, tiles, step),
        out_shape=(
            jax.ShapeDtypeStruct((blocks, frames, 128), F32),
            jax.ShapeDtypeStruct((n_dp, 8, 128), F32),
            jax.ShapeDtypeStruct((blocks, 8, 128), F32),
            jax.ShapeDtypeStruct((1,), jnp.int32),
            jax.ShapeDtypeStruct((8, 128), F32),
        ),
        in_specs=[smem, vmem, pl.BlockSpec(memory_space=pl.ANY)],
        out_specs=(vmem, vmem, vmem, smem, vmem),
        scratch_shapes=[
            pltpu.VMEM((total, frames, 2 * width), jnp.bfloat16),
            pltpu.VMEM((blocks, frames, 2 * width), jnp.bfloat16),
            pltpu.VMEM((blocks, frames, 128), F32),
            pltpu.VMEM((8, frames), F32),
            pltpu.SemaphoreType.DMA((total,)),
        ],
        name="first_pass",
    )(meta, student, every)


def second_kernel(tiles, step, meta, ok_ref, s_ref, every, row_ref, far_ref, own_ref, out_ref, t_buf, s_buf, w_buf, acc, sems):
    frames, width = s_ref.shape[1], s_ref.shape[2]
    total = 2 * tiles
    c2 = 1.0 / math.sqrt(width) / math.log(2.0)
    scale = 1.0 / math.sqrt(width)
    for e in range(total):
        fetch(meta, every, t_buf, sems, e).start()
    for a in range(2):
        s_buf[a, :, :width] = s_ref[a]
        augment(s_buf, a, meta[3 * total + a], False)
    acc[...] = jnp.zeros_like(acc)

    def lse_row(e, r):
        a, k = e // tiles, e % tiles
        far = far_ref[meta[2 * total + e], r:r + 1, :]
        return jnp.where(k == 0, own_ref[a, r:r + 1, :], far)

    def tile(e, carry):
        a = e // tiles
        keys = meta[total + e]
        fetch(meta, every, t_buf, sems, e).wait()
        augment(t_buf, e, keys, True)
        chunks = (meta[3 * total + a] + step - 1) // step
        spans = (keys + STEP - 1) // STEP
        for r in range(frames // 128):
            rows = slice(r * 128, (r + 1) * 128)
            weight = jnp.broadcast_to(0.5 * jnp.exp(-lse_row(e, r)), (128, 128)).T
            t = t_buf[e, rows, :width]
            w_buf[rows, :width] = t
            inside = lax.broadcasted_iota(jnp.int32, (128, 128), 0) + r * 128 < keys
            w_buf[rows, width:] = jnp.where(inside, weight * t.astype(F32), 0.0).astype(w_buf.dtype)
        for v in range(1, frames // STEP + 1):
            @pl.when(spans == v)
            def _():
                def chunk(i, c):
                    rows = pl.ds(pl.multiple_of(i * step, step), step)
                    lhs = s_buf[a, rows, :]
                    part = acc[a, rows, :]
                    for j in range(v):
                        cols = slice(j * STEP, (j + 1) * STEP)
                        p = jnp.exp2(nt(lhs, t_buf[e, cols, :]) * c2).astype(jnp.bfloat16)
                        part = part + jnp.dot(p, w_buf[cols, :], preferred_element_type=F32)
                    acc[a, rows, :] = part
                    return c
                lax.fori_loop(0, chunks, chunk, 0)
        return carry

    @pl.when(ok_ref[0] != 0)
    def _():
        lax.fori_loop(0, total, tile, 0)

    @pl.when(ok_ref[0] == 0)
    def _():
        half = 128

        def slow_tile(e, carry):
            a = e // tiles
            fetch(meta, every, t_buf, sems, e).wait()
            augment(t_buf, e, meta[total + e], True)

            def slow_chunk(i, c):
                rows = pl.ds(pl.multiple_of(i * half, half), half)
                lhs = s_buf[a, rows, :]
                part = acc[a, rows, width:]
                for j in range(frames // half):
                    cols = slice(j * half, (j + 1) * half)
                    sc = nt(lhs, t_buf[e, cols, :]) * scale
                    g = 0.5 * (jnp.exp(sc - row_ref[a, rows, :]) + jnp.exp(sc - lse_row(e, j)))
                    g = jnp.where(sc > -0.01 * BIG, g, 0.0)
                    part = part + jnp.dot(g.astype(jnp.bfloat16), t_buf[e, cols, :width], preferred_element_type=F32)
                acc[a, rows, width:] = part
                return c
            lax.fori_loop(0, frames // half, slow_chunk, 0)
            return carry
        lax.fori_loop(0, total, slow_tile, 0)

    for a in range(2):
        row = lax.broadcasted_iota(jnp.int32, (frames, width), 0)
        scaled = 0.5 * jnp.exp(-row_ref[a]) * acc[a, :, :width]
        grad = jnp.where(ok_ref[0] != 0, scaled, 0.0) + acc[a, :, width:] - t_buf[a * tiles, :, :width].astype(F32)
        out_ref[a] = jnp.where(row < meta[3 * total + a], grad * scale, 0.0).astype(out_ref.dtype)


def second_pass(meta, ok, student, every, rows, far, own, tiles, step=512):
    blocks, frames, width = student.shape
    total = blocks * tiles
    smem, vmem = pl.BlockSpec(memory_space=pltpu.SMEM), pl.BlockSpec(memory_space=pltpu.VMEM)
    return pl.pallas_call(
        functools.partial(second_kernel, tiles, step),
        out_shape=jax.ShapeDtypeStruct(student.shape, student.dtype),
        in_specs=[smem, smem, vmem, pl.BlockSpec(memory_space=pl.ANY), vmem, vmem, vmem],
        out_specs=vmem,
        scratch_shapes=[
            pltpu.VMEM((total, frames, 2 * width), jnp.bfloat16),
            pltpu.VMEM((blocks, frames, 2 * width), jnp.bfloat16),
            pltpu.VMEM((frames, 2 * width), jnp.bfloat16),
            pltpu.VMEM((blocks, frames, 2 * width), F32),
            pltpu.SemaphoreType.DMA((total,)),
        ],
        name="second_pass",
    )(meta, ok, student, every, rows, far, own)


def exchange_kernel(n_dp, n_tm, bias_ref, pick_ref, count_ref, send_ref, own_ref, sum_ref, far_ref, lse_ref, loss_ref,
                    inc, reply, side, column, s1, r1, s2, r2, s3, r3, s4, r4):
    me, tm = lax.axis_index("dp"), lax.axis_index("tm")
    barrier = pltpu.get_barrier_semaphore()

    def greet(o, c):
        pl.semaphore_signal(barrier, inc=1, device_id=((me + o) % n_dp, tm), device_id_type=MESH)
        return c
    lax.fori_loop(1, n_dp, greet, 0)
    for o in range(1, n_tm):
        pl.semaphore_signal(barrier, inc=1, device_id=(me, (tm + o) % n_tm), device_id_type=MESH)
    inc[me] = send_ref[me]
    pl.semaphore_wait(barrier, n_dp - 1 + n_tm - 1)

    def ask(o):
        to = (me + o) % n_dp
        return pltpu.make_async_remote_copy(
            src_ref=send_ref.at[to], dst_ref=inc.at[me], send_sem=s1.at[o], recv_sem=r1.at[o],
            device_id=(to, tm), device_id_type=MESH)

    def answer(o):
        to = (me + o) % n_dp
        return pltpu.make_async_remote_copy(
            src_ref=reply.at[to], dst_ref=far_ref.at[me], send_sem=s2.at[o], recv_sem=r2.at[o],
            device_id=(to, tm), device_id_type=MESH)

    def tell(o):
        return pltpu.make_async_remote_copy(
            src_ref=column.at[me], dst_ref=column.at[me], send_sem=s4.at[o], recv_sem=r4.at[o],
            device_id=((me + o) % n_dp, tm), device_id_type=MESH)

    def beside(o):
        return pltpu.make_async_remote_copy(
            src_ref=side.at[tm], dst_ref=side.at[tm], send_sem=s3.at[o], recv_sem=r3.at[o],
            device_id=(me, (tm + o) % n_tm), device_id_type=MESH)

    def each(f):
        def step(o, c):
            f(o)
            return c
        lax.fori_loop(1, n_dp, step, 0)

    each(lambda o: ask(o).start())
    each(lambda o: ask(o).wait_recv())
    terms = sum_ref[...]
    frame = lax.broadcasted_iota(jnp.int32, (8, 128), 0) * 128 + lax.broadcasted_iota(jnp.int32, (8, 128), 1)
    for a in range(2):
        best = own_ref[a]
        for p in range(n_dp):
            best = jnp.maximum(best, inc[p] + bias_ref[a, p])
        total = jnp.exp(own_ref[a] - best)
        for p in range(n_dp):
            total = total + jnp.exp(inc[p] + bias_ref[a, p] - best)
        lse = best + jnp.log(total)
        lse = jnp.where(frame < count_ref[a], lse, 0.0)
        lse_ref[a] = lse
        terms = terms + lse
    side[tm] = terms
    for p in range(n_dp):
        share = pick_ref[p]
        reply[p] = lse_ref[0] * (1.0 - share) + lse_ref[1] * share
    far_ref[me] = reply[me]
    each(lambda o: answer(o).start())
    for o in range(1, n_tm):
        beside(o).start()
    for o in range(1, n_tm):
        beside(o).wait_recv()
    rows = side[0]
    for t in range(1, n_tm):
        rows = rows + side[t]
    column[me] = rows
    each(lambda o: tell(o).start())
    each(lambda o: answer(o).wait_recv())
    each(lambda o: tell(o).wait_recv())
    rows = column[0]
    for p in range(1, n_dp):
        rows = rows + column[p]
    loss_ref[0] = 0.5 * jnp.sum(rows)
    each(lambda o: ask(o).wait_send())
    each(lambda o: answer(o).wait_send())
    each(lambda o: tell(o).wait_send())
    for o in range(1, n_tm):
        beside(o).wait_send()


def exchange(bias, pick, count, send, own, sums, n_tm):
    n_dp = send.shape[0]
    smem, vmem = pl.BlockSpec(memory_space=pltpu.SMEM), pl.BlockSpec(memory_space=pltpu.VMEM)
    dma = pltpu.SemaphoreType.DMA
    return pl.pallas_call(
        functools.partial(exchange_kernel, n_dp, n_tm),
        out_shape=(
            jax.ShapeDtypeStruct((n_dp, 8, 128), F32),
            jax.ShapeDtypeStruct((2, 8, 128), F32),
            jax.ShapeDtypeStruct((1,), F32),
        ),
        in_specs=[smem, smem, smem, vmem, vmem, vmem],
        out_specs=(vmem, vmem, smem),
        scratch_shapes=[
            pltpu.VMEM((n_dp, 8, 128), F32), pltpu.VMEM((n_dp, 8, 128), F32),
            pltpu.VMEM((n_tm, 8, 128), F32), pltpu.VMEM((n_dp, 8, 128), F32),
            dma((n_dp,)), dma((n_dp,)), dma((n_dp,)), dma((n_dp,)),
            dma((n_tm,)), dma((n_tm,)), dma((n_dp,)), dma((n_dp,)),
        ],
        compiler_params=pltpu.CompilerParams(collective_id=1, has_side_effects=True),
        name="exchange",
    )(bias, pick, count, send, own, sums)


def body(student, teacher, partner_dp, partner_slot, valid_frames):
    n_dp, n_tm = lax.axis_size("dp"), lax.axis_size("tm")
    me, tm = lax.axis_index("dp"), lax.axis_index("tm")
    blocks, frames, width = student.shape
    k = partner_dp.shape[1]
    entries = blocks * k
    dest_all = lax.dynamic_index_in_dim(partner_dp.reshape(n_dp, n_tm, entries), tm, 1, keepdims=False)
    slot_all = lax.dynamic_index_in_dim(partner_slot.reshape(n_dp, n_tm, entries), tm, 1, keepdims=False)
    lens = lax.dynamic_index_in_dim(valid_frames.reshape(n_dp, n_tm, blocks), tm, 1, keepdims=False)
    dest = lax.dynamic_index_in_dim(dest_all, me, 0, keepdims=False).reshape(blocks, k)
    slot = lax.dynamic_index_in_dim(slot_all, me, 0, keepdims=False).reshape(blocks, k)
    own = me * blocks + jnp.arange(blocks, dtype=jnp.int32)
    ids = jnp.concatenate([own[:, None], dest * blocks + slot], axis=1).reshape(-1)
    flat_lens = lens.reshape(-1)
    goes = jnp.concatenate([jnp.zeros((blocks, 1), jnp.int32), dest], axis=1).reshape(-1)
    count = lax.dynamic_index_in_dim(lens, me, 0, keepdims=False)
    meta = jnp.concatenate([ids, flat_lens[ids], goes, count])
    wanted = dest_all == me
    asked = jnp.max(jnp.where(wanted, slot_all, -1), axis=1)
    bias = jnp.where(asked[None] == jnp.arange(blocks, dtype=jnp.int32)[:, None], 0.0, -BIG).astype(F32)
    pick = jnp.maximum(asked, 0).astype(F32)

    every = gather(teacher, n_dp).reshape(n_dp * blocks, frames, width)
    rows, send, own_lse, ok, sums = first_pass(meta, student, every, n_dp, k + 1)
    far, lse, loss_sum = exchange(bias, pick, count, send, own_lse, sums, n_tm)
    grad = second_pass(meta, ok, student, every, rows, far, lse, k + 1)
    loss = loss_sum[0] / jnp.sum(valid_frames).astype(F32)
    return (loss, grad)


def solution(mesh):
    placed = (P(("dp", "tm"), None, None), P(("dp", "tm"), None, None), P(), P(), P())
    return jax.shard_map(
        body,
        mesh=mesh,
        in_specs=placed,
        out_specs=(P(), P(("dp", "tm"), None, None)),
        check_vma=False,
    )
```

```python
import functools
import heapq
import math

import jax
import jax.numpy as jnp
from jax import lax
from jax.experimental import pallas as pl
from jax.experimental.pallas import tpu as pltpu
from jax.sharding import PartitionSpec as P

MESH = pl.DeviceIdType.MESH
F32 = jnp.float32
BIG = 1e30

ZP, ZM, YP, YM = range(4)
MOVE = {ZP: (1, 0), ZM: (-1, 0), YP: (0, 1), YM: (0, -1)}


PARTS = 2


def onward(tile, oz, oy, part):
    half = part * 2 // PARTS
    first, second = (oz, oy) if tile == 0 else (oy, oz)
    plus1, minus1 = (ZP, ZM) if tile == 0 else (YP, YM)
    plus2, minus2 = (YP, YM) if tile == 0 else (ZP, ZM)
    links = []
    if second == 0:
        if first == 0:
            links += [plus1, minus1]
        elif first == 1 and half == 0:
            links += [plus1]
        elif first == 3 and half == 1:
            links += [minus1]
        links += [plus2, minus2]
    elif second == 1 and half == 0:
        links += [plus2]
    elif second == 3 and half == 1:
        links += [minus2]
    return links


def moved(oz, oy, link):
    dz, dy = MOVE[link]
    return (oz + dz) % 4, (oy + dy) % 4


def plan():
    free = [0.0] * 4
    events, order, count = [], [], 0

    def send(unit, link, now):
        nonlocal count
        tile, oz, oy, half = unit
        start = max(now, free[link])
        free[link] = start + 1.0
        noz, noy = moved(oz, oy, link)
        heapq.heappush(events, (free[link] + 0.5, count, (tile, noz, noy, half), link))
        count += 1

    first = []
    for link in range(4):
        near = 0 if link in (ZP, ZM) else 1
        lead = 0 if link in (ZP, YP) else 1
        for tile in (near, 1 - near):
            for part in range(PARTS):
                first.append(((tile, 0, 0, part if lead == 0 else PARTS - 1 - part), link))
    first = [first[k * 2 * PARTS + i] for i in range(2 * PARTS) for k in range(4)]
    for unit, link in first:
        send(unit, link, 0.0)
    while events:
        now, _, unit, _ = heapq.heappop(events)
        out = onward(*unit)
        order.append((unit, out))
        for link in out:
            send(unit, link, now)
    return first, order, max(free)


def lay_requests(me, tm, n_tm, dp_ref, slot_ref, ask_ref):
    asked = jnp.max(jnp.where(dp_ref[...] == me, slot_ref[...], -1).astype(F32), axis=0, keepdims=True)
    lane = lax.broadcasted_iota(jnp.int32, asked.shape, 1) // 2
    for p in range(ask_ref.shape[0]):
        one = jnp.max(jnp.where(lane == p * n_tm + tm, asked, -1.0), axis=1, keepdims=True)
        one = jnp.broadcast_to(one, (8, 128))
        ask_ref[p, 0] = jnp.where(one == 0.0, 0.0, -BIG)
        ask_ref[p, 1] = jnp.where(one == 1.0, 0.0, -BIG)
        ask_ref[p, 2] = jnp.maximum(one, 0.0)


def lay_side(me, tm, n_tm, t_ref, s_ref, valid_ref, side_ref):
    blocks, frames, width = t_ref.shape
    row = lax.broadcasted_iota(jnp.int32, (frames, width), 0)
    total = jnp.zeros((8, width), F32)
    for a in range(blocks):
        both = s_ref[a].astype(F32) * t_ref[a].astype(F32)
        both = jnp.where(row < valid_ref[(me * n_tm + tm) * blocks + a], both, 0.0)
        total = total + jnp.sum(both.reshape(frames // 8, 8, width), axis=0)
    side_ref[0] = total * (-2.0 / math.sqrt(width))
    count = lax.fori_loop(0, valid_ref.shape[0], lambda i, c: c + valid_ref[i], jnp.int32(0))
    side_ref[1] = jnp.full((8, width), count).astype(F32)


def gather_kernel(rows, n_tm, t_ref, s_ref, dp_ref, slot_ref, valid_ref, out_ref, ask_ref, side_ref,
                  send_sem, recv_sem, peer_send, peer_recv, own_sem):
    half_rows = rows // PARTS
    me, tm = lax.axis_index("dp"), lax.axis_index("tm")
    z, y, c = me // 8, (me // 2) % 4, me % 2

    def dp_of(zz, yy, cc):
        return (zz * 4 + yy) * 2 + cc

    near = [
        dp_of((z + 1) % 4, y, c), dp_of((z + 3) % 4, y, c),
        dp_of(z, (y + 1) % 4, c), dp_of(z, (y + 3) % 4, c),
    ]
    peer = dp_of(z, y, 1 - c)
    barrier = pltpu.get_barrier_semaphore()
    for other in near + [peer]:
        pl.semaphore_signal(barrier, inc=1, device_id=(other, tm), device_id_type=MESH)
    pl.semaphore_wait(barrier, 5)

    first, order, _ = plan()
    sends = []

    def recv_id(unit):
        tile, oz, oy, half = unit
        return ((tile * 4 + oz) * 4 + oy) * PARTS + half

    def slot(unit):
        _, oz, oy, _ = unit
        return dp_of((z + 4 - oz) % 4, (y + 4 - oy) % 4, c)

    def place(ref, unit):
        tile, oz, oy, half = unit
        return ref.at[slot(unit), tile, pl.ds(half * half_rows, half_rows)]

    def source(unit):
        tile, oz, oy, half = unit
        if oz == 0 and oy == 0:
            return t_ref.at[tile, pl.ds(half * half_rows, half_rows)]
        return place(out_ref, unit)

    def send(unit, link):
        tile, oz, oy, half = unit
        copy = pltpu.make_async_remote_copy(
            src_ref=source(unit), dst_ref=place(out_ref, unit),
            send_sem=send_sem.at[len(sends)], recv_sem=recv_sem.at[recv_id((tile, *moved(oz, oy, link), half))],
            device_id=(near[link], tm), device_id_type=MESH,
        )
        copy.start()
        sends.append(copy)

    shares = []

    def share(unit):
        copy = pltpu.make_async_remote_copy(
            src_ref=source(unit), dst_ref=place(out_ref, unit),
            send_sem=peer_send.at[recv_id(unit)], recv_sem=peer_recv.at[recv_id(unit)],
            device_id=(peer, tm), device_id_type=MESH,
        )
        copy.start()
        shares.append(copy)

    for unit, link in first:
        send(unit, link)
    for tile in (0, 1):
        for half in range(PARTS):
            share((tile, 0, 0, half))
    own = pltpu.make_async_copy(t_ref, out_ref.at[me], own_sem)
    own.start()
    lay_requests(me, tm, n_tm, dp_ref, slot_ref, ask_ref)
    lay_side(me, tm, n_tm, t_ref, s_ref, valid_ref, side_ref)
    for unit, out in order:
        here = place(out_ref, unit)
        pltpu.make_async_remote_copy(
            src_ref=here, dst_ref=here, send_sem=send_sem.at[0], recv_sem=recv_sem.at[recv_id(unit)],
            device_id=(near[0], tm), device_id_type=MESH,
        ).wait_recv()
        for link in out:
            send(unit, link)
        share(unit)
    for copy in shares:
        copy.wait_send()
        copy.wait_recv()
    for copy in sends:
        copy.wait_send()
    own.wait()


def gather(teacher, student, tables, n_dp, n_tm):
    blocks, rows, width = teacher.shape
    smem, vmem, far = (pl.BlockSpec(memory_space=m) for m in (pltpu.SMEM, pltpu.VMEM, pl.ANY))
    first, order, _ = plan()
    n_sends = len(first) + sum(len(o) for _, o in order)
    return pl.pallas_call(
        functools.partial(gather_kernel, rows, n_tm),
        out_shape=(
            jax.ShapeDtypeStruct((n_dp, blocks, rows, width), teacher.dtype),
            jax.ShapeDtypeStruct((n_dp, 3, 8, 128), F32),
            jax.ShapeDtypeStruct((2, 8, 128), F32),
        ),
        in_specs=[vmem, vmem, vmem, vmem, smem],
        out_specs=(far, vmem, vmem),
        scratch_shapes=[
            pltpu.SemaphoreType.DMA((n_sends,)), pltpu.SemaphoreType.DMA((32 * PARTS,)),
            pltpu.SemaphoreType.DMA((32 * PARTS,)), pltpu.SemaphoreType.DMA((32 * PARTS,)), pltpu.SemaphoreType.DMA,
        ],
        compiler_params=pltpu.CompilerParams(collective_id=0, has_side_effects=True),
        name="gather",
    )(teacher, student, *tables)


LOW, HIGH = 2.0 ** -60, 2.0 ** 100
SPAN = 256
UNIT = 256


def lay_table(meta, tiles, me, tm, n_tm, dp_ref, slot_ref, valid_ref):
    for a in range(2):
        mine = (me * n_tm + tm) * 2 + a
        meta[3, a] = valid_ref[mine]
        meta[0, a * tiles] = me * 2 + a
        meta[1, a * tiles] = valid_ref[mine]
        meta[2, a * tiles] = 0
        for k in range(1, tiles):
            far, slot = dp_ref[k - 1, mine], slot_ref[k - 1, mine]
            meta[0, a * tiles + k] = far * 2 + slot
            meta[1, a * tiles + k] = valid_ref[(far * n_tm + tm) * 2 + slot]
            meta[2, a * tiles + k] = far


def edge(shape, start, count, key):
    row = lax.broadcasted_iota(jnp.int32, shape, 0) + start
    lane = lax.broadcasted_iota(jnp.int32, shape, 1)
    mine, other = (0, 1) if key else (1, 0)
    return jnp.where(lane == mine, jnp.where(row < count, 0.0, -BIG), jnp.where(lane == other, 1.0, 0.0)).astype(jnp.bfloat16)


def nt(a, b):
    return lax.dot_general(a, b, (((1,), (1,)), ((), ())), preferred_element_type=F32)


def ceil_of(x, n):
    return (x + n - 1) // n


def stash(e, u, v, inside, outside, sems, out):
    rows = pl.ds(pl.multiple_of(u * UNIT, UNIT), UNIT)
    near, far = inside.at[e, pl.ds(0, v), rows], outside.at[e, pl.ds(0, v), rows]
    return pltpu.make_async_copy(near, far, sems.at[e, u]) if out else pltpu.make_async_copy(far, near, sems.at[e, u])


def first_kernel(tiles, n_tm, dp_ref, slot_ref, valid_ref, s_ref, every, row_ref, send_ref, own_ref, ok_ref, sum_ref, e_hbm,
                 t_buf, right, key_edge, key_full, acc, col, ends, e_buf, meta, sems, e_sems):
    me, tm = lax.axis_index("dp"), lax.axis_index("tm")
    frames, width = s_ref.shape[1], s_ref.shape[2]
    total = 2 * tiles
    spans_most = frames // SPAN
    scale = 1.0 / math.sqrt(width)
    c2 = scale / math.log(2.0)
    lay_table(meta, tiles, me, tm, n_tm, dp_ref, slot_ref, valid_ref)

    def fetch(e):
        return pltpu.make_async_copy(every.at[meta[0, e]], t_buf.at[e], sems.at[e])
    for e in range(total):
        fetch(e).start()
    for a in range(2):
        right[a] = edge((frames, width), 0, meta[3, a], False)
    key_full[...] = edge((SPAN, width), 0, SPAN, True)
    acc[...] = jnp.zeros_like(acc)
    ok_ref[0] = 1
    sum_ref[...] = jnp.zeros_like(sum_ref)
    ends[...] = jnp.ones_like(ends)
    lane = lax.broadcasted_iota(jnp.int32, (1, frames), 1)
    send_ref[...] = jnp.zeros_like(send_ref)

    def put(e, values):
        a, k = e // tiles, e % tiles

        @pl.when(k == 0)
        def _():
            for r in range(8):
                own_ref[a, r:r + 1, :] = values[:, r * 128:(r + 1) * 128]

        @pl.when(k != 0)
        def _():
            for r in range(8):
                send_ref[meta[2, e], r:r + 1, :] = values[:, r * 128:(r + 1) * 128]

    def by_spans(e, run):
        spans = ceil_of(meta[1, e], SPAN)
        for v in range(1, spans_most + 1):
            pl.when(spans == v)(functools.partial(run, v))

    def tile(e, carry):
        a = e // tiles
        keys = meta[1, e]
        fetch(e).wait()
        col[...] = jnp.zeros_like(col)
        units = ceil_of(meta[3, a], UNIT)
        key_edge[...] = edge((SPAN, width), (ceil_of(keys, SPAN) - 1) * SPAN, keys, True)

        def run(v):
            def piece(u, many):
                n = UNIT * many
                rows = pl.ds(pl.multiple_of(u * UNIT, UNIT), n)
                lhs = jnp.concatenate([s_ref[a, rows, :], right[a, rows, :]], axis=1)
                part = acc[a, rows, :]
                for j in range(v):
                    cols = slice(j * SPAN, (j + 1) * SPAN)
                    side = key_edge if j == v - 1 else key_full
                    rhs = jnp.concatenate([t_buf[e, cols, :], side[...]], axis=1)
                    p = jnp.exp2(nt(lhs, rhs) * c2)
                    e_buf[e, j, rows, :] = p.astype(jnp.bfloat16)
                    for w in range(SPAN // 128):
                        part = part + p[:, w * 128:(w + 1) * 128]
                    col[:, cols] += jnp.sum(p.reshape(n // 8, 8, SPAN), axis=0)
                acc[a, rows, :] = part
                for i in range(many):
                    stash(e, u + i, v, e_buf, e_hbm, e_sems, True).start()

            def pair(i, c):
                piece(2 * i, 2)
                return c
            lax.fori_loop(0, units // 2, pair, 0)
            pl.when(units % 2 == 1)(lambda: piece(units - 1, 1))
        by_spans(e, run)
        sums = jnp.sum(col[...], axis=0, keepdims=True)
        sums = jnp.where(lane < keys, sums, 1.0)
        ends[0:1, :] = jnp.minimum(ends[0:1, :], sums)
        ends[1:2, :] = jnp.maximum(ends[1:2, :], sums)
        put(e, jnp.where(lane < keys, jnp.log(sums), -BIG))
        return carry

    lax.fori_loop(0, total, tile, 0)

    low, high = jnp.min(ends[0:1, :]), jnp.max(ends[1:2, :])
    row = lax.broadcasted_iota(jnp.int32, (frames, 128), 0)
    for a in range(2):
        sums = jnp.broadcast_to(jnp.sum(acc[a], axis=1, keepdims=True), (frames, 128))
        sums = jnp.where(row < meta[3, a], sums, 1.0)
        low, high = jnp.minimum(low, jnp.min(sums)), jnp.maximum(high, jnp.max(sums))
        lse = jnp.log(sums)
        row_ref[a] = lse
        sum_ref[...] += jnp.sum(lse.reshape(frames // 8, 8, 128), axis=0)

    @pl.when(jnp.logical_not((low >= LOW) & (high <= HIGH)))
    def _():
        ok_ref[0] = 0
        row_ref[...] = jnp.full(row_ref.shape, -BIG, F32)
        acc[...] = jnp.zeros_like(acc)
        sum_ref[...] = jnp.zeros_like(sum_ref)
        half = 128

        def slow_tile(e, carry):
            a = e // tiles
            keys = meta[1, e]
            col[0:1, :] = jnp.full((1, frames), -BIG, F32)
            col[1:2, :] = jnp.zeros((1, frames), F32)

            def slow_chunk(i, c):
                rows = pl.ds(pl.multiple_of(i * half, half), half)
                lhs = jnp.concatenate([s_ref[a, rows, :], right[a, rows, :]], axis=1)
                for j in range(frames // half):
                    cols = slice(j * half, (j + 1) * half)
                    rhs = jnp.concatenate([t_buf[e, cols, :], edge((half, width), j * half, keys, True)], axis=1)
                    sc = nt(lhs, rhs) * scale
                    old = row_ref[a, rows, :]
                    new = jnp.maximum(old, jnp.broadcast_to(jnp.max(sc, axis=1, keepdims=True), (half, 128)))
                    acc[a, rows, :] = acc[a, rows, :] * jnp.exp(old - new) + jnp.broadcast_to(
                        jnp.sum(jnp.where(sc > -0.01 * BIG, jnp.exp(sc - new[:, :1]), 0.0), axis=1, keepdims=True), (half, 128))
                    row_ref[a, rows, :] = new
                    cold = col[0:1, cols]
                    cnew = jnp.maximum(cold, jnp.max(sc, axis=0, keepdims=True))
                    col[1:2, cols] = col[1:2, cols] * jnp.exp(cold - cnew) + jnp.sum(
                        jnp.where(sc > -0.01 * BIG, jnp.exp(sc - cnew), 0.0), axis=0, keepdims=True)
                    col[0:1, cols] = cnew
                return c
            lax.fori_loop(0, frames // half, slow_chunk, 0)
            real = lane < keys
            put(e, jnp.where(real, col[0:1, :] + jnp.log(jnp.where(real, col[1:2, :], 1.0)), -BIG))
            return carry
        lax.fori_loop(0, total, slow_tile, 0)
        for a in range(2):
            lse = jnp.where(row < meta[3, a], row_ref[a] + jnp.log(jnp.maximum(acc[a], 1e-30)), 0.0)
            row_ref[a] = lse
            sum_ref[...] += jnp.sum(lse.reshape(frames // 8, 8, 128), axis=0)

    sum_ref[...] = sum_ref[...] * (1.0 / 128)

    def drain(e, carry):
        def run(v):
            def one(u, c):
                stash(e, u, v, e_buf, e_hbm, e_sems, True).wait()
                return c
            lax.fori_loop(0, ceil_of(meta[3, e // tiles], UNIT), one, 0)
        by_spans(e, run)
        return carry
    lax.fori_loop(0, total, drain, 0)


def first_pass(tables, student, every, n_dp, n_tm, tiles):
    blocks, frames, width = student.shape
    total = blocks * tiles
    smem, vmem, far = (pl.BlockSpec(memory_space=m) for m in (pltpu.SMEM, pltpu.VMEM, pl.ANY))
    return pl.pallas_call(
        functools.partial(first_kernel, tiles, n_tm),
        out_shape=(
            jax.ShapeDtypeStruct((blocks, frames, 128), F32),
            jax.ShapeDtypeStruct((n_dp, 8, 128), F32),
            jax.ShapeDtypeStruct((blocks, 8, 128), F32),
            jax.ShapeDtypeStruct((1,), jnp.int32),
            jax.ShapeDtypeStruct((8, 128), F32),
            jax.ShapeDtypeStruct((total, frames // SPAN, frames, SPAN), jnp.bfloat16),
        ),
        in_specs=[smem, smem, smem, vmem, far],
        out_specs=(vmem, vmem, vmem, smem, vmem, far),
        scratch_shapes=[
            pltpu.VMEM((total, frames, width), jnp.bfloat16),
            pltpu.VMEM((blocks, frames, width), jnp.bfloat16),
            pltpu.VMEM((SPAN, width), jnp.bfloat16),
            pltpu.VMEM((SPAN, width), jnp.bfloat16),
            pltpu.VMEM((blocks, frames, 128), F32),
            pltpu.VMEM((8, frames), F32),
            pltpu.VMEM((8, frames), F32),
            pltpu.VMEM((total, frames // SPAN, frames, SPAN), jnp.bfloat16),
            pltpu.SMEM((4, total), jnp.int32),
            pltpu.SemaphoreType.DMA((total,)),
            pltpu.SemaphoreType.DMA((total, frames // UNIT)),
        ],
        compiler_params=pltpu.CompilerParams(vmem_limit_bytes=60 * 1024 * 1024),
        name="first_pass",
    )(*tables, student, every)


def second_kernel(tiles, n_tm, dp_ref, slot_ref, valid_ref, ok_ref, s_ref, every, e_hbm, row_ref, far_ref, own_ref, out_ref,
                  w_buf, acc, e_buf, meta, sems, e_sems):
    me, tm = lax.axis_index("dp"), lax.axis_index("tm")
    frames, width = s_ref.shape[1], s_ref.shape[2]
    total = 2 * tiles
    spans_most = frames // SPAN
    scale = 1.0 / math.sqrt(width)
    lay_table(meta, tiles, me, tm, n_tm, dp_ref, slot_ref, valid_ref)

    def fetch(e):
        return pltpu.make_async_copy(every.at[meta[0, e]], w_buf.at[e, :, pl.ds(0, width)], sems.at[e])

    def by_spans(e, run):
        spans = ceil_of(meta[1, e], SPAN)
        for v in range(1, spans_most + 1):
            pl.when(spans == v)(functools.partial(run, v))

    def load(e, carry):
        fetch(e).start()

        @pl.when(ok_ref[0] != 0)
        def _():
            def run(v):
                def one(u, c):
                    stash(e, u, v, e_buf, e_hbm, e_sems, False).start()
                    return c
                lax.fori_loop(0, ceil_of(meta[3, e // tiles], UNIT), one, 0)
            by_spans(e, run)
        return carry
    lax.fori_loop(0, total, load, 0)
    acc[...] = jnp.zeros_like(acc)

    def lse_row(e, r):
        a, k = e // tiles, e % tiles
        return jnp.where(k == 0, own_ref[a, r:r + 1, :], far_ref[meta[2, e], r:r + 1, :])

    def tile(e, carry):
        a = e // tiles
        units = ceil_of(meta[3, a], UNIT)
        fetch(e).wait()

        def run(v):
            for r in range(v * SPAN // 128):
                rows = slice(r * 128, (r + 1) * 128)
                weight = jnp.broadcast_to(0.5 * jnp.exp(-lse_row(e, r)), (128, 128)).T
                w_buf[e, rows, width:] = (weight * w_buf[e, rows, :width].astype(F32)).astype(w_buf.dtype)

            def piece(u, many):
                for i in range(many):
                    stash(e, u + i, v, e_buf, e_hbm, e_sems, False).wait()
                rows = pl.ds(pl.multiple_of(u * UNIT, UNIT), UNIT * many)
                lhs = jnp.concatenate([e_buf[e, j, rows, :] for j in range(v)], axis=1)
                acc[a, rows, :] += jnp.dot(lhs, w_buf[e, :v * SPAN, :], preferred_element_type=F32)

            def pair(i, c):
                piece(2 * i, 2)
                return c
            lax.fori_loop(0, units // 2, pair, 0)
            pl.when(units % 2 == 1)(lambda: piece(units - 1, 1))
        by_spans(e, run)
        return carry

    @pl.when(ok_ref[0] != 0)
    def _():
        lax.fori_loop(0, total, tile, 0)

    @pl.when(ok_ref[0] == 0)
    def _():
        half = 128

        def slow_tile(e, carry):
            a = e // tiles
            fetch(e).wait()

            def slow_chunk(i, c):
                rows = pl.ds(pl.multiple_of(i * half, half), half)
                part = acc[a, rows, width:]
                for j in range(frames // half):
                    t = w_buf[e, j * half:(j + 1) * half, :width]
                    inside = lax.broadcasted_iota(jnp.int32, (half, half), 1) + j * half < meta[1, e]
                    sc = nt(s_ref[a, rows, :], t) * scale
                    g = 0.5 * (jnp.exp(jnp.where(inside, sc - row_ref[a, rows, :], -BIG))
                               + jnp.exp(jnp.where(inside, sc - lse_row(e, j), -BIG)))
                    part = part + jnp.dot(g.astype(jnp.bfloat16), t, preferred_element_type=F32)
                acc[a, rows, width:] = part
                return c
            lax.fori_loop(0, ceil_of(meta[3, a], half), slow_chunk, 0)
            return carry
        lax.fori_loop(0, total, slow_tile, 0)

    row = lax.broadcasted_iota(jnp.int32, (frames, width), 0)
    for a in range(2):
        scaled = 0.5 * jnp.exp(-row_ref[a]) * acc[a, :, :width]
        grad = jnp.where(ok_ref[0] != 0, scaled, 0.0) + acc[a, :, width:] - w_buf[a * tiles, :, :width].astype(F32)
        out_ref[a] = jnp.where(row < meta[3, a], grad * scale, 0.0).astype(out_ref.dtype)


def second_pass(tables, ok, student, every, kept, rows, far, own, n_tm, tiles):
    blocks, frames, width = student.shape
    total = blocks * tiles
    smem, vmem, hbm = (pl.BlockSpec(memory_space=m) for m in (pltpu.SMEM, pltpu.VMEM, pl.ANY))
    return pl.pallas_call(
        functools.partial(second_kernel, tiles, n_tm),
        out_shape=jax.ShapeDtypeStruct(student.shape, student.dtype),
        in_specs=[smem, smem, smem, smem, vmem, hbm, hbm, vmem, vmem, vmem],
        out_specs=vmem,
        scratch_shapes=[
            pltpu.VMEM((total, frames, 2 * width), jnp.bfloat16),
            pltpu.VMEM((blocks, frames, 2 * width), F32),
            pltpu.VMEM((total, frames // SPAN, frames, SPAN), jnp.bfloat16),
            pltpu.SMEM((4, total), jnp.int32),
            pltpu.SemaphoreType.DMA((total,)),
            pltpu.SemaphoreType.DMA((total, frames // UNIT)),
        ],
        compiler_params=pltpu.CompilerParams(vmem_limit_bytes=60 * 1024 * 1024),
        name="second_pass",
    )(*tables, ok, student, every, kept, rows, far, own)


def exchange_kernel(n_dp, n_tm, valid_ref, ask_ref, side_ref, send_ref, own_ref, sum_ref, far_ref, lse_ref, loss_ref,
                    inc, reply, across, column, s1, r1, s2, r2, s3, r3, s4, r4):
    me, tm = lax.axis_index("dp"), lax.axis_index("tm")
    others = [(me + o) % n_dp for o in range(1, n_dp)]
    beside = [(tm + o) % n_tm for o in range(1, n_tm)]
    barrier = pltpu.get_barrier_semaphore()
    for to in others:
        pl.semaphore_signal(barrier, inc=1, device_id=(to, tm), device_id_type=MESH)
    for to in beside:
        pl.semaphore_signal(barrier, inc=1, device_id=(me, to), device_id_type=MESH)
    inc[me] = send_ref[me]
    pl.semaphore_wait(barrier, n_dp - 1 + n_tm - 1)

    def ship(src, dst, sent, got, where):
        pltpu.make_async_remote_copy(
            src_ref=src, dst_ref=dst, send_sem=sent, recv_sem=got, device_id=where, device_id_type=MESH).start()

    def settle(buf, sem, count):
        part = buf.at[pl.ds(0, count)]
        pltpu.make_async_copy(part, part, sem).wait()

    for to in others:
        ship(send_ref.at[to], inc.at[me], s1, r1, (to, tm))
    settle(inc, r1, n_dp - 1)
    terms = sum_ref[...] + side_ref[0]
    frame = lax.broadcasted_iota(jnp.int32, (8, 128), 0) * 128 + lax.broadcasted_iota(jnp.int32, (8, 128), 1)
    for a in range(2):
        best = own_ref[a]
        for p in range(n_dp):
            best = jnp.maximum(best, inc[p] + ask_ref[p, a])
        total = jnp.exp(own_ref[a] - best)
        for p in range(n_dp):
            total = total + jnp.exp(inc[p] + ask_ref[p, a] - best)
        lse = jnp.where(frame < valid_ref[(me * n_tm + tm) * 2 + a], best + jnp.log(total), 0.0)
        lse_ref[a] = lse
        terms = terms + lse
    across[tm] = terms
    for p in range(n_dp):
        share = ask_ref[p, 2]
        reply[p] = lse_ref[0] * (1.0 - share) + lse_ref[1] * share
    far_ref[me] = reply[me]
    for to in beside:
        ship(across.at[tm], across.at[tm], s3, r3, (me, to))
    for to in others:
        ship(reply.at[to], far_ref.at[me], s2, r2, (to, tm))
    settle(across, r3, n_tm - 1)
    rows = across[0]
    for t in range(1, n_tm):
        rows = rows + across[t]
    column[me] = rows
    for to in others:
        ship(column.at[me], column.at[me], s4, r4, (to, tm))
    settle(far_ref, r2, n_dp - 1)
    settle(column, r4, n_dp - 1)
    rows = column[0]
    for p in range(1, n_dp):
        rows = rows + column[p]
    loss_ref[...] = jnp.broadcast_to(
        0.5 * jnp.sum(jnp.sum(rows, axis=0, keepdims=True), axis=1, keepdims=True), (8, 128)) / side_ref[1]
    settle(send_ref, s1, n_dp - 1)
    settle(reply, s2, n_dp - 1)
    settle(across, s3, n_tm - 1)
    settle(column, s4, n_dp - 1)


def exchange(valid, ask, side, send, own, sums, n_tm):
    n_dp = send.shape[0]
    smem, vmem = pl.BlockSpec(memory_space=pltpu.SMEM), pl.BlockSpec(memory_space=pltpu.VMEM)
    return pl.pallas_call(
        functools.partial(exchange_kernel, n_dp, n_tm),
        out_shape=(
            jax.ShapeDtypeStruct((n_dp, 8, 128), F32),
            jax.ShapeDtypeStruct((2, 8, 128), F32),
            jax.ShapeDtypeStruct((8, 128), F32),
        ),
        in_specs=[smem] + [vmem] * 5,
        out_specs=(vmem, vmem, vmem),
        scratch_shapes=[
            pltpu.VMEM((n_dp, 8, 128), F32), pltpu.VMEM((n_dp, 8, 128), F32),
            pltpu.VMEM((n_tm, 8, 128), F32), pltpu.VMEM((n_dp, 8, 128), F32),
        ] + [pltpu.SemaphoreType.DMA] * 8,
        compiler_params=pltpu.CompilerParams(collective_id=1, has_side_effects=True),
        name="exchange",
    )(valid, ask, side, send, own, sums)


def body(student, teacher, partner_dp, partner_slot, valid_frames):
    n_dp, n_tm = lax.axis_size("dp"), lax.axis_size("tm")
    blocks, frames, width = student.shape
    tiles = partner_dp.shape[1] + 1
    tables = (partner_dp.T, partner_slot.T, valid_frames)
    every, ask, side = gather(teacher, student, tables, n_dp, n_tm)
    every = every.reshape(n_dp * blocks, frames, width)
    rows, send, own, ok, sums, kept = first_pass(tables, student, every, n_dp, n_tm, tiles)
    far, lse, loss = exchange(valid_frames, ask, side, send, own, sums, n_tm)
    grad = second_pass(tables, ok, student, every, kept, rows, far, lse, n_tm, tiles)
    return (loss[0, 0], grad)


def solution(mesh):
    placed = (P(("dp", "tm"), None, None), P(("dp", "tm"), None, None), P(), P(), P())
    return jax.shard_map(
        body,
        mesh=mesh,
        in_specs=placed,
        out_specs=(P(), P(("dp", "tm"), None, None)),
        check_vma=False,
    )
```

```python
import functools
import heapq
import math

import jax
import jax.numpy as jnp
from jax import lax
from jax.experimental import pallas as pl
from jax.experimental.pallas import tpu as pltpu
from jax.sharding import PartitionSpec as P

MESH = pl.DeviceIdType.MESH
F32 = jnp.float32
BIG = 1e30

ZP, ZM, YP, YM = range(4)
MOVE = {ZP: (1, 0), ZM: (-1, 0), YP: (0, 1), YM: (0, -1)}


PARTS = 2


def onward(tile, oz, oy, part):
    half = part * 2 // PARTS
    first, second = (oz, oy) if tile == 0 else (oy, oz)
    plus1, minus1 = (ZP, ZM) if tile == 0 else (YP, YM)
    plus2, minus2 = (YP, YM) if tile == 0 else (ZP, ZM)
    links = []
    if second == 0:
        if first == 0:
            links += [plus1, minus1]
        elif first == 1 and half == 0:
            links += [plus1]
        elif first == 3 and half == 1:
            links += [minus1]
        links += [plus2, minus2]
    elif second == 1 and half == 0:
        links += [plus2]
    elif second == 3 and half == 1:
        links += [minus2]
    return links


def moved(oz, oy, link):
    dz, dy = MOVE[link]
    return (oz + dz) % 4, (oy + dy) % 4


def plan():
    free = [0.0] * 4
    events, order, count = [], [], 0

    def send(unit, link, now):
        nonlocal count
        tile, oz, oy, half = unit
        start = max(now, free[link])
        free[link] = start + 1.0
        noz, noy = moved(oz, oy, link)
        heapq.heappush(events, (free[link] + 0.5, count, (tile, noz, noy, half), link))
        count += 1

    first = []
    for link in range(4):
        near = 0 if link in (ZP, ZM) else 1
        lead = 0 if link in (ZP, YP) else 1
        for tile in (near, 1 - near):
            for part in range(PARTS):
                first.append(((tile, 0, 0, part if lead == 0 else PARTS - 1 - part), link))
    first = [first[k * 2 * PARTS + i] for i in range(2 * PARTS) for k in range(4)]
    for unit, link in first:
        send(unit, link, 0.0)
    while events:
        now, _, unit, _ = heapq.heappop(events)
        out = onward(*unit)
        order.append((unit, out))
        for link in out:
            send(unit, link, now)
    return first, order, max(free)


def lay_requests(me, tm, n_tm, dp_ref, slot_ref, ask_ref):
    asked = jnp.max(jnp.where(dp_ref[...] == me, slot_ref[...], -1).astype(F32), axis=0, keepdims=True)
    lane = lax.broadcasted_iota(jnp.int32, asked.shape, 1) // 2
    for p in range(ask_ref.shape[0]):
        one = jnp.max(jnp.where(lane == p * n_tm + tm, asked, -1.0), axis=1, keepdims=True)
        one = jnp.broadcast_to(one, (8, 128))
        ask_ref[p, 0] = jnp.where(one == 0.0, 0.0, -BIG)
        ask_ref[p, 1] = jnp.where(one == 1.0, 0.0, -BIG)
        ask_ref[p, 2] = jnp.maximum(one, 0.0)


def lay_side(me, tm, n_tm, t_ref, s_ref, valid_ref, side_ref):
    blocks, frames, width = t_ref.shape
    row = lax.broadcasted_iota(jnp.int32, (frames, width), 0)
    total = jnp.zeros((8, width), F32)
    for a in range(blocks):
        both = s_ref[a].astype(F32) * t_ref[a].astype(F32)
        both = jnp.where(row < valid_ref[(me * n_tm + tm) * blocks + a], both, 0.0)
        total = total + jnp.sum(both.reshape(frames // 8, 8, width), axis=0)
    side_ref[0] = total * (-2.0 / math.sqrt(width))
    count = lax.fori_loop(0, valid_ref.shape[0], lambda i, c: c + valid_ref[i], jnp.int32(0))
    side_ref[1] = 0.5 / jnp.full((8, width), count).astype(F32)


def settle(buf, sem, count):
    part = buf.at[pl.ds(0, count)]
    pltpu.make_async_copy(part, part, sem).wait()


def gather_kernel(rows, n_tm, t_ref, s_ref, dp_ref, slot_ref, valid_ref, out_ref, ask_ref, side_ref,
                  send_sem, recv_sem, peer_send, peer_recv, own_sem):
    half_rows = rows // PARTS
    me, tm = lax.axis_index("dp"), lax.axis_index("tm")
    z, y, c = me // 8, (me // 2) % 4, me % 2

    def dp_of(zz, yy, cc):
        return (zz * 4 + yy) * 2 + cc

    near = [
        dp_of((z + 1) % 4, y, c), dp_of((z + 3) % 4, y, c),
        dp_of(z, (y + 1) % 4, c), dp_of(z, (y + 3) % 4, c),
    ]
    peer = dp_of(z, y, 1 - c)
    barrier = pltpu.get_barrier_semaphore()
    for other in near + [peer]:
        pl.semaphore_signal(barrier, inc=1, device_id=(other, tm), device_id_type=MESH)
    pl.semaphore_wait(barrier, 5)

    first, order, _ = plan()

    def recv_id(unit):
        tile, oz, oy, half = unit
        return ((tile * 4 + oz) * 4 + oy) * PARTS + half

    def slot(unit):
        _, oz, oy, _ = unit
        return dp_of((z + 4 - oz) % 4, (y + 4 - oy) % 4, c)

    def place(ref, unit):
        tile, oz, oy, half = unit
        return ref.at[slot(unit), tile, pl.ds(half * half_rows, half_rows)]

    def source(unit):
        tile, oz, oy, half = unit
        if oz == 0 and oy == 0:
            return t_ref.at[tile, pl.ds(half * half_rows, half_rows)]
        return place(out_ref, unit)

    def send(unit, link):
        tile, oz, oy, half = unit
        copy = pltpu.make_async_remote_copy(
            src_ref=source(unit), dst_ref=place(out_ref, unit),
            send_sem=send_sem, recv_sem=recv_sem.at[recv_id((tile, *moved(oz, oy, link), half))],
            device_id=(near[link], tm), device_id_type=MESH,
        )
        copy.start()

    def share(unit):
        copy = pltpu.make_async_remote_copy(
            src_ref=source(unit), dst_ref=place(out_ref, unit),
            send_sem=peer_send, recv_sem=peer_recv,
            device_id=(peer, tm), device_id_type=MESH,
        )
        copy.start()

    for unit, link in first:
        send(unit, link)
    for tile in (0, 1):
        for half in range(PARTS):
            share((tile, 0, 0, half))
    own = pltpu.make_async_copy(t_ref, out_ref.at[me], own_sem)
    own.start()
    lay_requests(me, tm, n_tm, dp_ref, slot_ref, ask_ref)
    lay_side(me, tm, n_tm, t_ref, s_ref, valid_ref, side_ref)
    for unit, out in order:
        here = place(out_ref, unit)
        pltpu.make_async_remote_copy(
            src_ref=here, dst_ref=here, send_sem=send_sem, recv_sem=recv_sem.at[recv_id(unit)],
            device_id=(near[0], tm), device_id_type=MESH,
        ).wait_recv()
        for link in out:
            send(unit, link)
        share(unit)
    settle(out_ref, peer_send, 16)
    settle(out_ref, peer_recv, 16)
    settle(out_ref, send_sem, 15)
    own.wait()


def gather(teacher, student, tables, n_dp, n_tm):
    blocks, rows, width = teacher.shape
    smem, vmem, far = (pl.BlockSpec(memory_space=m) for m in (pltpu.SMEM, pltpu.VMEM, pl.ANY))
    return pl.pallas_call(
        functools.partial(gather_kernel, rows, n_tm),
        out_shape=(
            jax.ShapeDtypeStruct((n_dp, blocks, rows, width), teacher.dtype),
            jax.ShapeDtypeStruct((n_dp, 3, 8, 128), F32),
            jax.ShapeDtypeStruct((2, 8, 128), F32),
        ),
        in_specs=[vmem, vmem, vmem, vmem, smem],
        out_specs=(far, vmem, vmem),
        scratch_shapes=[
            pltpu.SemaphoreType.DMA, pltpu.SemaphoreType.DMA((32 * PARTS,)),
            pltpu.SemaphoreType.DMA, pltpu.SemaphoreType.DMA, pltpu.SemaphoreType.DMA,
        ],
        compiler_params=pltpu.CompilerParams(collective_id=0, has_side_effects=True),
        name="gather",
    )(teacher, student, *tables)


LOW, HIGH = 2.0 ** -60, 2.0 ** 100
SPAN = 256
UNIT = 256


def lay_table(meta, tiles, me, tm, n_tm, dp_ref, slot_ref, valid_ref):
    for a in range(2):
        mine = (me * n_tm + tm) * 2 + a
        meta[3, a] = valid_ref[mine]
        meta[0, a * tiles] = me * 2 + a
        meta[1, a * tiles] = valid_ref[mine]
        meta[2, a * tiles] = 0
        for k in range(1, tiles):
            far, slot = dp_ref[k - 1, mine], slot_ref[k - 1, mine]
            meta[0, a * tiles + k] = far * 2 + slot
            meta[1, a * tiles + k] = valid_ref[(far * n_tm + tm) * 2 + slot]
            meta[2, a * tiles + k] = far


def edge(shape, start, count, key):
    row = lax.broadcasted_iota(jnp.int32, shape, 0) + start
    lane = lax.broadcasted_iota(jnp.int32, shape, 1)
    mine, other = (0, 1) if key else (1, 0)
    return jnp.where(lane == mine, jnp.where(row < count, 0.0, -BIG), jnp.where(lane == other, 1.0, 0.0)).astype(jnp.bfloat16)


def nt(a, b):
    return lax.dot_general(a, b, (((1,), (1,)), ((), ())), preferred_element_type=F32)


def ceil_of(x, n):
    return (x + n - 1) // n


def stash(e, v, m, inside, outside, sems, out):
    rows = pl.ds(0, m * UNIT)
    near, far = inside.at[e, pl.ds(0, v), rows], outside.at[e, pl.ds(0, v), rows]
    return pltpu.make_async_copy(near, far, sems.at[e]) if out else pltpu.make_async_copy(far, near, sems.at[e])


def by_shape(keys, count, most, run):
    spans, units = ceil_of(keys, SPAN), ceil_of(count, UNIT)
    for v in range(1, most + 1):
        @pl.when(spans == v)
        def _():
            for m in range(1, most + 1):
                pl.when(units == m)(functools.partial(run, v, m))


def first_kernel(tiles, n_tm, dp_ref, slot_ref, valid_ref, s_ref, every, row_ref, send_ref, own_ref, ok_ref, sum_ref, e_hbm,
                 s_buf, row_buf, t_buf, right, key_edge, key_full, acc, col, ends, e_buf, meta, sems, e_sems, out_sem):
    me, tm = lax.axis_index("dp"), lax.axis_index("tm")
    frames, width = s_ref.shape[1], s_ref.shape[2]
    total = 2 * tiles
    spans_most = frames // SPAN
    scale = 1.0 / math.sqrt(width)
    c2 = scale / math.log(2.0)
    bring = pltpu.make_async_copy(s_ref, s_buf, out_sem)
    bring.start()
    lay_table(meta, tiles, me, tm, n_tm, dp_ref, slot_ref, valid_ref)

    def fetch(e):
        return pltpu.make_async_copy(every.at[meta[0, e]], t_buf.at[e], sems.at[e])
    for e in range(total):
        fetch(e).start()
    for a in range(2):
        right[a] = edge((frames, width), 0, meta[3, a], False)
    key_full[...] = edge((SPAN, width), 0, SPAN, True)
    acc[...] = jnp.zeros_like(acc)
    ok_ref[0] = 1
    sum_ref[...] = jnp.zeros_like(sum_ref)
    ends[...] = jnp.ones_like(ends)
    lane = lax.broadcasted_iota(jnp.int32, (1, frames), 1)
    send_ref[...] = jnp.zeros_like(send_ref)

    def put(e, values):
        a, k = e // tiles, e % tiles

        @pl.when(k == 0)
        def _():
            for r in range(8):
                own_ref[a, r:r + 1, :] = values[:, r * 128:(r + 1) * 128]

        @pl.when(k != 0)
        def _():
            for r in range(8):
                send_ref[meta[2, e], r:r + 1, :] = values[:, r * 128:(r + 1) * 128]

    def tile(e, carry):
        a = e // tiles
        keys = meta[1, e]
        fetch(e).wait()
        key_edge[...] = edge((SPAN, width), (ceil_of(keys, SPAN) - 1) * SPAN, keys, True)

        def run(v, m):
            n = UNIT * m
            lhs = jnp.concatenate([s_buf[a, :n, :], right[a, :n, :]], axis=1)
            part = acc[a, :n, :]
            for j in range(v):
                cols = slice(j * SPAN, (j + 1) * SPAN)
                side = key_edge if j == v - 1 else key_full
                rhs = jnp.concatenate([t_buf[e, cols, :], side[...]], axis=1)
                p = jnp.exp2(nt(lhs, rhs) * c2)
                e_buf[e, j, :n, :] = p.astype(jnp.bfloat16)
                for w in range(SPAN // 128):
                    part = part + p[:, w * 128:(w + 1) * 128]
                col[:, cols] = jnp.sum(p.reshape(n // 8, 8, SPAN), axis=0)
            acc[a, :n, :] = part
            stash(e, v, m, e_buf, e_hbm, e_sems, True).start()
        by_shape(keys, meta[3, a], spans_most, run)
        sums = jnp.sum(col[...], axis=0, keepdims=True)
        sums = jnp.where(lane < keys, sums, 1.0)
        ends[0:1, :] = jnp.minimum(ends[0:1, :], sums)
        ends[1:2, :] = jnp.maximum(ends[1:2, :], sums)
        put(e, jnp.where(lane < keys, jnp.log(sums), -BIG))
        return carry

    bring.wait()
    lax.fori_loop(0, total, tile, 0)

    low, high = jnp.min(ends[0:1, :]), jnp.max(ends[1:2, :])
    row = lax.broadcasted_iota(jnp.int32, (frames, 128), 0)
    for a in range(2):
        sums = jnp.broadcast_to(jnp.sum(acc[a], axis=1, keepdims=True), (frames, 128))
        sums = jnp.where(row < meta[3, a], sums, 1.0)
        low, high = jnp.minimum(low, jnp.min(sums)), jnp.maximum(high, jnp.max(sums))
        row_buf[a] = (0.5 * scale) / sums
        sum_ref[...] += jnp.sum(jnp.log(sums).reshape(frames // 8, 8, 128), axis=0)

    @pl.when(jnp.logical_not((low >= LOW) & (high <= HIGH)))
    def _():
        ok_ref[0] = 0
        row_buf[...] = jnp.full(row_buf.shape, -BIG, F32)
        acc[...] = jnp.zeros_like(acc)
        sum_ref[...] = jnp.zeros_like(sum_ref)
        half = 128

        def slow_tile(e, carry):
            a = e // tiles
            keys = meta[1, e]
            col[0:1, :] = jnp.full((1, frames), -BIG, F32)
            col[1:2, :] = jnp.zeros((1, frames), F32)

            def slow_chunk(i, c):
                rows = pl.ds(pl.multiple_of(i * half, half), half)
                lhs = jnp.concatenate([s_buf[a, rows, :], right[a, rows, :]], axis=1)
                for j in range(frames // half):
                    cols = slice(j * half, (j + 1) * half)
                    rhs = jnp.concatenate([t_buf[e, cols, :], edge((half, width), j * half, keys, True)], axis=1)
                    sc = nt(lhs, rhs) * scale
                    old = row_buf[a, rows, :]
                    new = jnp.maximum(old, jnp.broadcast_to(jnp.max(sc, axis=1, keepdims=True), (half, 128)))
                    acc[a, rows, :] = acc[a, rows, :] * jnp.exp(old - new) + jnp.broadcast_to(
                        jnp.sum(jnp.where(sc > -0.01 * BIG, jnp.exp(sc - new[:, :1]), 0.0), axis=1, keepdims=True), (half, 128))
                    row_buf[a, rows, :] = new
                    cold = col[0:1, cols]
                    cnew = jnp.maximum(cold, jnp.max(sc, axis=0, keepdims=True))
                    col[1:2, cols] = col[1:2, cols] * jnp.exp(cold - cnew) + jnp.sum(
                        jnp.where(sc > -0.01 * BIG, jnp.exp(sc - cnew), 0.0), axis=0, keepdims=True)
                    col[0:1, cols] = cnew
                return c
            lax.fori_loop(0, frames // half, slow_chunk, 0)
            real = lane < keys
            put(e, jnp.where(real, col[0:1, :] + jnp.log(jnp.where(real, col[1:2, :], 1.0)), -BIG))
            return carry
        lax.fori_loop(0, total, slow_tile, 0)
        for a in range(2):
            lse = jnp.where(row < meta[3, a], row_buf[a] + jnp.log(jnp.maximum(acc[a], 1e-30)), 0.0)
            row_buf[a] = lse
            sum_ref[...] += jnp.sum(lse.reshape(frames // 8, 8, 128), axis=0)

    sum_ref[...] = sum_ref[...] * (1.0 / 128)

    give = pltpu.make_async_copy(row_buf, row_ref, out_sem)
    give.start()

    def drain(e, carry):
        by_shape(meta[1, e], meta[3, e // tiles], spans_most, lambda v, m: stash(e, v, m, e_buf, e_hbm, e_sems, True).wait())
        return carry
    lax.fori_loop(0, total, drain, 0)
    give.wait()


def first_pass(tables, student, every, n_dp, n_tm, tiles):
    blocks, frames, width = student.shape
    total = blocks * tiles
    smem, vmem, far = (pl.BlockSpec(memory_space=m) for m in (pltpu.SMEM, pltpu.VMEM, pl.ANY))
    return pl.pallas_call(
        functools.partial(first_kernel, tiles, n_tm),
        out_shape=(
            jax.ShapeDtypeStruct((blocks, frames, 128), F32),
            jax.ShapeDtypeStruct((n_dp, 8, 128), F32),
            jax.ShapeDtypeStruct((blocks, 8, 128), F32),
            jax.ShapeDtypeStruct((1,), jnp.int32),
            jax.ShapeDtypeStruct((8, 128), F32),
            jax.ShapeDtypeStruct((total, frames // SPAN, frames, SPAN), jnp.bfloat16),
        ),
        in_specs=[smem, smem, smem, far, far],
        out_specs=(far, vmem, vmem, smem, vmem, far),
        scratch_shapes=[
            pltpu.VMEM((blocks, frames, width), jnp.bfloat16),
            pltpu.VMEM((blocks, frames, 128), F32),
            pltpu.VMEM((total, frames, width), jnp.bfloat16),
            pltpu.VMEM((blocks, frames, width), jnp.bfloat16),
            pltpu.VMEM((SPAN, width), jnp.bfloat16),
            pltpu.VMEM((SPAN, width), jnp.bfloat16),
            pltpu.VMEM((blocks, frames, 128), F32),
            pltpu.VMEM((8, frames), F32),
            pltpu.VMEM((8, frames), F32),
            pltpu.VMEM((total, frames // SPAN, frames, SPAN), jnp.bfloat16),
            pltpu.SMEM((4, total), jnp.int32),
            pltpu.SemaphoreType.DMA((total,)),
            pltpu.SemaphoreType.DMA((total,)),
            pltpu.SemaphoreType.DMA,
        ],
        compiler_params=pltpu.CompilerParams(vmem_limit_bytes=60 * 1024 * 1024),
        name="first_pass",
    )(*tables, student, every)


def second_kernel(tiles, n_tm, dp_ref, slot_ref, valid_ref, ok_ref, s_ref, every, e_hbm, row_ref, far_ref, own_ref, out_ref,
                  s_buf, row_buf, w_buf, acc, e_buf, meta, sems, e_sems, row_sem, s_sem):
    me, tm = lax.axis_index("dp"), lax.axis_index("tm")
    frames, width = s_ref.shape[1], s_ref.shape[2]
    total = 2 * tiles
    spans_most = frames // SPAN
    scale = 1.0 / math.sqrt(width)
    lay_table(meta, tiles, me, tm, n_tm, dp_ref, slot_ref, valid_ref)

    def fetch(e):
        return pltpu.make_async_copy(every.at[meta[0, e]], w_buf.at[e, :, pl.ds(0, width)], sems.at[e])

    def load(e, carry):
        fetch(e).start()

        @pl.when(ok_ref[0] != 0)
        def _():
            by_shape(meta[1, e], meta[3, e // tiles], spans_most,
                     lambda v, m: stash(e, v, m, e_buf, e_hbm, e_sems, False).start())
        return carry
    lax.fori_loop(0, total, load, 0)
    rows_in = pltpu.make_async_copy(row_ref, row_buf, row_sem)
    rows_in.start()
    acc[...] = jnp.zeros_like(acc)

    def lse_row(e, r):
        a, k = e // tiles, e % tiles
        return jnp.where(k == 0, own_ref[a, r:r + 1, :], far_ref[meta[2, e], r:r + 1, :])

    def tile(e, carry):
        a = e // tiles
        fetch(e).wait()

        def run(v, m):
            n = UNIT * m
            for r in range(v * SPAN // 128):
                rows = slice(r * 128, (r + 1) * 128)
                weight = jnp.broadcast_to((0.5 * scale) * jnp.exp(-lse_row(e, r)), (128, 128)).T
                w_buf[e, rows, width:] = (weight * w_buf[e, rows, :width].astype(F32)).astype(w_buf.dtype)
            stash(e, v, m, e_buf, e_hbm, e_sems, False).wait()
            lhs = jnp.concatenate([e_buf[e, j, :n, :] for j in range(v)], axis=1)
            acc[a, :n, :] += jnp.dot(lhs, w_buf[e, :v * SPAN, :], preferred_element_type=F32)
        by_shape(meta[1, e], meta[3, a], spans_most, run)
        return carry

    @pl.when(ok_ref[0] != 0)
    def _():
        lax.fori_loop(0, total, tile, 0)

    @pl.when(ok_ref[0] == 0)
    def _():
        half = 128
        students = pltpu.make_async_copy(s_ref, s_buf, s_sem)
        students.start()
        students.wait()

        def slow_tile(e, carry):
            a = e // tiles
            fetch(e).wait()

            def slow_chunk(i, c):
                rows = pl.ds(pl.multiple_of(i * half, half), half)
                part = acc[a, rows, width:]
                for j in range(frames // half):
                    t = w_buf[e, j * half:(j + 1) * half, :width]
                    inside = lax.broadcasted_iota(jnp.int32, (half, half), 1) + j * half < meta[1, e]
                    sc = nt(s_buf[a, rows, :], t) * scale
                    g = 0.5 * (jnp.exp(jnp.where(inside, sc - row_buf[a, rows, :], -BIG))
                               + jnp.exp(jnp.where(inside, sc - lse_row(e, j), -BIG)))
                    part = part + scale * jnp.dot(g.astype(jnp.bfloat16), t, preferred_element_type=F32)
                acc[a, rows, width:] = part
                return c
            lax.fori_loop(0, ceil_of(meta[3, a], half), slow_chunk, 0)
            return carry
        lax.fori_loop(0, total, slow_tile, 0)
        acc[:, :, :width] = jnp.zeros_like(acc[:, :, :width])

    rows_in.wait()
    row = lax.broadcasted_iota(jnp.int32, (frames, width), 0)
    for a in range(2):
        grad = row_buf[a] * acc[a, :, :width] + acc[a, :, width:] - scale * w_buf[a * tiles, :, :width].astype(F32)
        out_ref[a] = jnp.where(row < meta[3, a], grad, 0.0).astype(out_ref.dtype)


def second_pass(tables, ok, student, every, kept, rows, far, own, n_tm, tiles):
    blocks, frames, width = student.shape
    total = blocks * tiles
    smem, vmem, hbm = (pl.BlockSpec(memory_space=m) for m in (pltpu.SMEM, pltpu.VMEM, pl.ANY))
    return pl.pallas_call(
        functools.partial(second_kernel, tiles, n_tm),
        out_shape=jax.ShapeDtypeStruct(student.shape, student.dtype),
        in_specs=[smem, smem, smem, smem, hbm, hbm, hbm, hbm, vmem, vmem],
        out_specs=vmem,
        scratch_shapes=[
            pltpu.VMEM((blocks, frames, width), jnp.bfloat16),
            pltpu.VMEM((blocks, frames, 128), F32),
            pltpu.VMEM((total, frames, 2 * width), jnp.bfloat16),
            pltpu.VMEM((blocks, frames, 2 * width), F32),
            pltpu.VMEM((total, frames // SPAN, frames, SPAN), jnp.bfloat16),
            pltpu.SMEM((4, total), jnp.int32),
            pltpu.SemaphoreType.DMA((total,)),
            pltpu.SemaphoreType.DMA((total,)),
            pltpu.SemaphoreType.DMA,
            pltpu.SemaphoreType.DMA,
        ],
        compiler_params=pltpu.CompilerParams(vmem_limit_bytes=60 * 1024 * 1024),
        name="second_pass",
    )(*tables, ok, student, every, kept, rows, far, own)


def exchange_kernel(n_dp, n_tm, valid_ref, ask_ref, side_ref, send_ref, own_ref, sum_ref, far_ref, lse_ref, loss_ref,
                    inc, reply, across, column, s1, r1, s2, r2, s3, r3, s4, r4):
    me, tm = lax.axis_index("dp"), lax.axis_index("tm")
    others = [(me + o) % n_dp for o in range(1, n_dp)]
    beside = [(tm + o) % n_tm for o in range(1, n_tm)]
    barrier = pltpu.get_barrier_semaphore()
    for to in others:
        pl.semaphore_signal(barrier, inc=1, device_id=(to, tm), device_id_type=MESH)
    for to in beside:
        pl.semaphore_signal(barrier, inc=1, device_id=(me, to), device_id_type=MESH)
    inc[me] = send_ref[me]
    pl.semaphore_wait(barrier, n_dp - 1 + n_tm - 1)

    def ship(src, dst, sent, got, where):
        pltpu.make_async_remote_copy(
            src_ref=src, dst_ref=dst, send_sem=sent, recv_sem=got, device_id=where, device_id_type=MESH).start()

    for to in others:
        ship(send_ref.at[to], inc.at[me], s1, r1, (to, tm))
    settle(inc, r1, n_dp - 1)
    terms = sum_ref[...] + side_ref[0]
    frame = lax.broadcasted_iota(jnp.int32, (8, 128), 0) * 128 + lax.broadcasted_iota(jnp.int32, (8, 128), 1)
    for a in range(2):
        best = own_ref[a]
        for p in range(n_dp):
            best = jnp.maximum(best, inc[p] + ask_ref[p, a])
        total = jnp.exp(own_ref[a] - best)
        for p in range(n_dp):
            total = total + jnp.exp(inc[p] + ask_ref[p, a] - best)
        lse = jnp.where(frame < valid_ref[(me * n_tm + tm) * 2 + a], best + jnp.log(total), 0.0)
        lse_ref[a] = lse
        terms = terms + lse
    across[tm] = terms
    for p in range(n_dp):
        share = ask_ref[p, 2]
        reply[p] = lse_ref[0] * (1.0 - share) + lse_ref[1] * share
    far_ref[me] = reply[me]
    for to in beside:
        ship(across.at[tm], across.at[tm], s3, r3, (me, to))
    for to in others:
        ship(reply.at[to], far_ref.at[me], s2, r2, (to, tm))
    settle(across, r3, n_tm - 1)
    rows = across[0]
    for t in range(1, n_tm):
        rows = rows + across[t]
    column[me] = rows
    for to in others:
        ship(column.at[me], column.at[me], s4, r4, (to, tm))
    settle(far_ref, r2, n_dp - 1)
    settle(column, r4, n_dp - 1)
    rows = column[0]
    for p in range(1, n_dp):
        rows = rows + column[p]
    loss_ref[0] = jnp.sum(rows * side_ref[1])
    settle(send_ref, s1, n_dp - 1)
    settle(reply, s2, n_dp - 1)
    settle(across, s3, n_tm - 1)
    settle(column, s4, n_dp - 1)


def exchange(valid, ask, side, send, own, sums, n_tm):
    n_dp = send.shape[0]
    smem, vmem = pl.BlockSpec(memory_space=pltpu.SMEM), pl.BlockSpec(memory_space=pltpu.VMEM)
    return pl.pallas_call(
        functools.partial(exchange_kernel, n_dp, n_tm),
        out_shape=(
            jax.ShapeDtypeStruct((n_dp, 8, 128), F32),
            jax.ShapeDtypeStruct((2, 8, 128), F32),
            jax.ShapeDtypeStruct((1,), F32),
        ),
        in_specs=[smem] + [vmem] * 5,
        out_specs=(vmem, vmem, smem),
        scratch_shapes=[
            pltpu.VMEM((n_dp, 8, 128), F32), pltpu.VMEM((n_dp, 8, 128), F32),
            pltpu.VMEM((n_tm, 8, 128), F32), pltpu.VMEM((n_dp, 8, 128), F32),
        ] + [pltpu.SemaphoreType.DMA] * 8,
        compiler_params=pltpu.CompilerParams(collective_id=1, has_side_effects=True),
        name="exchange",
    )(valid, ask, side, send, own, sums)


def body(student, teacher, partner_dp, partner_slot, valid_frames):
    n_dp, n_tm = lax.axis_size("dp"), lax.axis_size("tm")
    blocks, frames, width = student.shape
    tiles = partner_dp.shape[1] + 1
    tables = (partner_dp.T, partner_slot.T, valid_frames)
    every, ask, side = gather(teacher, student, tables, n_dp, n_tm)
    every = every.reshape(n_dp * blocks, frames, width)
    rows, send, own, ok, sums, kept = first_pass(tables, student, every, n_dp, n_tm, tiles)
    far, lse, loss = exchange(valid_frames, ask, side, send, own, sums, n_tm)
    grad = second_pass(tables, ok, student, every, kept, rows, far, lse, n_tm, tiles)
    return (loss[0], grad)


def solution(mesh):
    placed = (P(("dp", "tm"), None, None), P(("dp", "tm"), None, None), P(), P(), P())
    return jax.shard_map(
        body,
        mesh=mesh,
        in_specs=placed,
        out_specs=(P(), P(("dp", "tm"), None, None)),
        check_vma=False,
    )
```

```python
import functools
import heapq
import math

import jax
import jax.numpy as jnp
from jax import lax
from jax.experimental import pallas as pl
from jax.experimental.pallas import tpu as pltpu
from jax.sharding import PartitionSpec as P

MESH = pl.DeviceIdType.MESH
F32 = jnp.float32
BIG = 1e30

PARTS = 2
ZP, ZM, YP, YM = range(4)
MOVE = {ZP: (1, 0), ZM: (-1, 0), YP: (0, 1), YM: (0, -1)}
FIRST = ((0, 0), (0, 1), (0, 3), (1, 0), (3, 0), (2, 0), (1, 1), (3, 1), (0, 2), (1, 3), (3, 3))
NEXT = ((2, 1), (2, 3))
LAST = ((1, 2), (3, 2), (2, 2))
CHIPS = FIRST + NEXT + LAST
EARLY = 10
SURE = 6
STARTED = 2 + EARLY


def onward(tile, oz, oy, part):
    half = part * 2 // PARTS
    first, second = (oz, oy) if tile == 0 else (oy, oz)
    plus1, minus1 = (ZP, ZM) if tile == 0 else (YP, YM)
    plus2, minus2 = (YP, YM) if tile == 0 else (ZP, ZM)
    links = []
    if second == 0:
        if first == 0:
            links += [plus1, minus1]
        elif first == 1 and half == 0:
            links += [plus1]
        elif first == 3 and half == 1:
            links += [minus1]
        links += [plus2, minus2]
    elif second == 1 and half == 0:
        links += [plus2]
    elif second == 3 and half == 1:
        links += [minus2]
    return links


def moved(oz, oy, link):
    dz, dy = MOVE[link]
    return (oz + dz) % 4, (oy + dy) % 4


def plan():
    free = [0.0] * 4
    events, order, count = [], [], 0

    def send(unit, link, now):
        nonlocal count
        tile, oz, oy, part = unit
        free[link] = max(now, free[link]) + 1.0
        noz, noy = moved(oz, oy, link)
        heapq.heappush(events, (free[link] + 0.5, count, (tile, noz, noy, part), link))
        count += 1

    first = []
    for link in range(4):
        near = 0 if link in (ZP, ZM) else 1
        lead = 0 if link in (ZP, YP) else 1
        for tile in (near, 1 - near):
            for part in range(PARTS):
                first.append(((tile, 0, 0, part if lead == 0 else PARTS - 1 - part), link))
    first = [first[k * 2 * PARTS + i] for i in range(2 * PARTS) for k in range(4)]
    for unit, link in first:
        send(unit, link, 0.0)
    while events:
        now, _, unit, _ = heapq.heappop(events)
        out = onward(*unit)
        order.append((unit, out))
        for link in out:
            send(unit, link, now)
    return first, order


def lay_requests(me, tm, n_tm, dp_ref, slot_ref, ask_ref):
    asked = jnp.max(jnp.where(dp_ref[...] == me, slot_ref[...], -1).astype(F32), axis=0, keepdims=True)
    lane = lax.broadcasted_iota(jnp.int32, asked.shape, 1) // 2
    for p in range(ask_ref.shape[0]):
        one = jnp.max(jnp.where(lane == p * n_tm + tm, asked, -1.0), axis=1, keepdims=True)
        one = jnp.broadcast_to(one, (8, 128))
        ask_ref[p, 0] = jnp.where(one == 0.0, 0.0, -BIG)
        ask_ref[p, 1] = jnp.where(one == 1.0, 0.0, -BIG)
        ask_ref[p, 2] = jnp.maximum(one, 0.0)


def lay_side(me, tm, n_tm, t_ref, s_ref, valid_ref, side_ref):
    blocks, frames, width = t_ref.shape
    row = lax.broadcasted_iota(jnp.int32, (frames, width), 0)
    total = jnp.zeros((8, width), F32)
    for a in range(blocks):
        both = s_ref[a].astype(F32) * t_ref[a].astype(F32)
        both = jnp.where(row < valid_ref[(me * n_tm + tm) * blocks + a], both, 0.0)
        total = total + jnp.sum(both.reshape(frames // 8, 8, width), axis=0)
    side_ref[0] = total * (-2.0 / math.sqrt(width))
    count = lax.fori_loop(0, valid_ref.shape[0], lambda i, c: c + valid_ref[i], jnp.int32(0))
    side_ref[1] = 0.5 / jnp.full((8, width), count).astype(F32)


def settle(buf, sem, count):
    part = buf.at[pl.ds(0, count)]
    pltpu.make_async_copy(part, part, sem).wait()


def gather_kernel(n_tm, t_ref, s_ref, dpv_ref, slotv_ref, dp_ref, slot_ref, valid_ref,
                  out_ref, e_hbm, acc_hbm, ask_hbm, side_ref, order_ref, col_ref,
                  first_buf, next_buf, e_buf, acc, right, ask, found_at, rank_at,
                  send_sem, recv_sem, peer_send, peer_recv, own_sem, out_sem, e_sem, more_sem):
    frames, width = t_ref.shape[1], t_ref.shape[2]
    n = frames // PARTS
    me, tm = lax.axis_index("dp"), lax.axis_index("tm")
    z, y, c = me // 8, (me // 2) % 4, me % 2
    c2 = 1.0 / math.sqrt(width) / math.log(2.0)

    def dp_of(zz, yy, cc):
        return (zz * 4 + yy) * 2 + cc

    def device_of(oz, oy, cc):
        return dp_of((z + 4 - oz) % 4, (y + 4 - oy) % 4, cc)

    near = [
        dp_of((z + 1) % 4, y, c), dp_of((z + 3) % 4, y, c),
        dp_of(z, (y + 1) % 4, c), dp_of(z, (y + 3) % 4, c),
    ]
    peer = dp_of(z, y, 1 - c)
    barrier = pltpu.get_barrier_semaphore()
    for other in near + [peer]:
        pl.semaphore_signal(barrier, inc=1, device_id=(other, tm), device_id_type=MESH)
    pl.semaphore_wait(barrier, 5)

    def recv_id(unit):
        tile, oz, oy, part = unit
        return ((tile * 4 + oz) * 4 + oy) * PARTS + part

    def device_store(oz, oy, cc):
        if (oz, oy) in FIRST:
            return first_buf.at[FIRST.index((oz, oy)) * 2 + cc]
        if (oz, oy) in NEXT:
            return next_buf.at[NEXT.index((oz, oy)) * 2 + cc]
        return out_ref.at[device_of(oz, oy, cc)]

    def place(unit):
        tile, oz, oy, part = unit
        return device_store(oz, oy, c).at[tile, pl.ds(part * n, n)]

    def source(unit):
        tile, oz, oy, part = unit
        return t_ref.at[tile, pl.ds(part * n, n)] if (oz, oy) == (0, 0) else place(unit)

    def onto(unit, link):
        tile, oz, oy, part = unit
        noz, noy = moved(oz, oy, link)
        if (noz, noy) in LAST:
            return out_ref.at[device_of(oz, oy, c), tile, pl.ds(part * n, n)]
        return place((tile, noz, noy, part))

    def send(unit, link):
        tile, oz, oy, part = unit
        pltpu.make_async_remote_copy(
            src_ref=source(unit), dst_ref=onto(unit, link),
            send_sem=send_sem, recv_sem=recv_sem.at[recv_id((tile, *moved(oz, oy, link), part))],
            device_id=(near[link], tm), device_id_type=MESH,
        ).start()

    def group(oz, oy):
        return 0 if (oz, oy) in FIRST else 1 if (oz, oy) in NEXT else 2

    def share(unit):
        pltpu.make_async_remote_copy(
            src_ref=source(unit), dst_ref=place(unit),
            send_sem=peer_send, recv_sem=peer_recv.at[group(unit[1], unit[2])],
            device_id=(peer, tm), device_id_type=MESH,
        ).start()

    def keep(oz, oy, cc):
        pltpu.make_async_copy(device_store(oz, oy, cc), out_ref.at[device_of(oz, oy, cc)], out_sem).start()

    first, order = plan()
    for unit, link in first:
        send(unit, link)
    for tile in (0, 1):
        for part in range(PARTS):
            share((tile, 0, 0, part))
    own = pltpu.make_async_copy(t_ref, device_store(0, 0, c), own_sem)
    own.start()
    pltpu.make_async_copy(t_ref, out_ref.at[me], out_sem).start()

    mine = (me * n_tm + tm) * 2
    partners = dp_ref.shape[0]

    def lay_order():
        names = [dp_ref[k, mine + a] for a in range(2) for k in range(partners)]
        rank = jnp.int32(0)
        for q in range(2 * len(CHIPS)):
            p = device_of(*CHIPS[q // 2], q % 2)
            found = jnp.int32(0)
            for j, name in enumerate(names):
                found = jnp.where(name == p, j + 1, found)
            found_at[q] = found
            rank_at[q] = jnp.where(found > 0, rank, -1)
            rank = rank + jnp.where(found > 0, 1, 0)
        where_ = []
        for r in range(2 * partners):
            at, entry = jnp.int32(0), jnp.int32(0)
            for q in range(r, r + 2 * partners + 1):
                if q < 2 * len(CHIPS):
                    hit = rank_at[q] == r
                    at = jnp.where(hit, q, at)
                    entry = jnp.where(hit, found_at[q] - 1, entry)
            order_ref[r] = entry
            where_.append(at)
        return where_

    def score(pos, a, keys, load, own_block):
        lhs = jnp.concatenate([s_ref[a], right[a]], axis=1)
        part = jnp.zeros((frames, 128), F32)
        for j in range(frames // SPAN):
            rhs = jnp.concatenate([load(slice(j * SPAN, (j + 1) * SPAN)), edge((SPAN, width), j * SPAN, keys, True)], axis=1)
            p = jnp.exp2(nt(lhs, rhs) * c2)
            e_buf[pos, j] = p.astype(jnp.bfloat16)
            for w in range(SPAN // 128):
                part = part + p[:, w * 128:(w + 1) * 128]
            sums = jnp.sum(p, axis=0, keepdims=True)
            for w in range(SPAN // 128):
                r = j * (SPAN // 128) + w
                col_ref[pos, r:r + 1, :] = sums[:, w * 128:(w + 1) * 128]
        if own_block:
            acc[a] = part
        else:
            for b in range(2):
                acc[b] += jnp.where(a == b, part, 0.0)
        pltpu.make_async_copy(e_buf.at[pos], e_hbm.at[pos], e_sem).start()

    def score_own(a):
        score(a, a, valid_ref[mine + a], lambda rows: t_ref[a, rows, :], True)

    def score_early(r, at):
        entry = order_ref[r]
        a, k = entry // partners, entry % partners
        slot = slot_ref[k, mine + a]
        keys = valid_ref[(dp_ref[k, mine + a] * n_tm + tm) * 2 + slot]
        many = 2 * len(FIRST)

        def load(rows):
            block = first_buf[jnp.minimum(at, many - 1), slot, rows, :]
            if r < SURE:
                return block
            later = next_buf[jnp.clip(at - many, 0, 2 * len(NEXT) - 1), slot, rows, :]
            return jnp.where(at < many, block, later)
        score(2 + r, a, keys, load, False)

    right[0] = edge((frames, width), 0, valid_ref[mine], False)
    right[1] = edge((frames, width), 0, valid_ref[mine + 1], False)
    lay_requests(me, tm, n_tm, dpv_ref, slotv_ref, ask)
    asks = pltpu.make_async_copy(ask, ask_hbm, more_sem.at[0])
    asks.start()
    at = lay_order()
    spots = [unit[1:3] for unit, _ in order]
    first_done = max(i for i, s in enumerate(spots) if s in FIRST)
    next_done = max(i for i, s in enumerate(spots) if s in NEXT)
    work = {4: lambda: lay_side(me, tm, n_tm, t_ref, s_ref, valid_ref, side_ref),
            6: lambda: score_own(0), 12: lambda: score_own(1)}
    missing = {chip: 2 * PARTS for chip in CHIPS}
    waiting = []
    for i, (unit, out) in enumerate(order):
        here = place(unit)
        pltpu.make_async_remote_copy(
            src_ref=here, dst_ref=here, send_sem=send_sem, recv_sem=recv_sem.at[recv_id(unit)],
            device_id=(near[0], tm), device_id_type=MESH,
        ).wait_recv()
        for link in out:
            send(unit, link)
        share(unit)
        chip = unit[1:3]
        missing[chip] -= 1
        if missing[chip] == 0 and chip not in LAST:
            keep(*chip, c)
        if i in work:
            work[i]()
        if i == first_done + 1:
            own.wait()
            settle(first_buf, peer_recv.at[0], len(FIRST))
            for chip in FIRST:
                keep(*chip, 1 - c)
            waiting += list(range(SURE))
        if i == next_done + 1:
            settle(next_buf, peer_recv.at[1], len(NEXT))
            for chip in NEXT:
                keep(*chip, 1 - c)
            waiting += list(range(SURE, EARLY))
        if waiting:
            r = waiting.pop(0)
            score_early(r, at[r])
    for r in waiting:
        score_early(r, at[r])
    sums = pltpu.make_async_copy(acc, acc_hbm, more_sem.at[1])
    sums.start()
    settle(out_ref, peer_recv.at[2], len(LAST))
    settle(out_ref, peer_send, len(CHIPS))
    settle(out_ref, send_sem, len(CHIPS) - 1)
    settle(out_ref, out_sem, 2 * (len(FIRST) + len(NEXT)))
    settle(e_hbm, e_sem, STARTED)
    asks.wait()
    sums.wait()


def gather(teacher, student, tables, n_dp, n_tm):
    blocks, frames, width = teacher.shape
    smem, vmem, far = (pl.BlockSpec(memory_space=m) for m in (pltpu.SMEM, pltpu.VMEM, pl.ANY))
    kept = (STARTED, frames // SPAN, frames, SPAN)
    dma = pltpu.SemaphoreType.DMA
    return pl.pallas_call(
        functools.partial(gather_kernel, n_tm),
        out_shape=(
            jax.ShapeDtypeStruct((n_dp, blocks, frames, width), teacher.dtype),
            jax.ShapeDtypeStruct(kept, jnp.bfloat16),
            jax.ShapeDtypeStruct((blocks, frames, 128), F32),
            jax.ShapeDtypeStruct((n_dp, 3, 8, 128), F32),
            jax.ShapeDtypeStruct((2, 8, 128), F32),
            jax.ShapeDtypeStruct((blocks * tables[0].shape[0],), jnp.int32),
            jax.ShapeDtypeStruct((STARTED, 8, 128), F32),
        ),
        in_specs=[vmem, vmem, vmem, vmem, smem, smem, smem],
        out_specs=(far, far, far, far, vmem, smem, vmem),
        scratch_shapes=[
            pltpu.VMEM((2 * len(FIRST), blocks, frames, width), teacher.dtype),
            pltpu.VMEM((2 * len(NEXT), blocks, frames, width), teacher.dtype),
            pltpu.VMEM(kept, jnp.bfloat16),
            pltpu.VMEM((blocks, frames, 128), F32),
            pltpu.VMEM((blocks, frames, width), jnp.bfloat16),
            pltpu.VMEM((n_dp, 3, 8, 128), F32),
            pltpu.SMEM((2 * len(CHIPS),), jnp.int32),
            pltpu.SMEM((2 * len(CHIPS),), jnp.int32),
            dma, dma((32 * PARTS,)), dma, dma((3,)), dma, dma, dma, dma((2,)),
        ],
        compiler_params=pltpu.CompilerParams(
            collective_id=0, has_side_effects=True, vmem_limit_bytes=60 * 1024 * 1024),
        name="gather",
    )(teacher, student, tables[0], tables[1], *tables)


LOW, HIGH = 2.0 ** -60, 2.0 ** 100
SPAN = 256
UNIT = 256


def lay_table(meta, tiles, me, tm, n_tm, dp_ref, slot_ref, valid_ref, order_ref):
    mine = (me * n_tm + tm) * 2
    for e in range(2 * tiles):
        if e < 2:
            a, far, slot = e, me, e
        else:
            entry = order_ref[e - 2]
            a, k = entry // (tiles - 1), entry % (tiles - 1)
            far, slot = dp_ref[k, mine + a], slot_ref[k, mine + a]
        meta[0, e] = far * 2 + slot
        meta[1, e] = valid_ref[(far * n_tm + tm) * 2 + slot]
        meta[2, e] = far
        meta[3, e] = a
        meta[4, e] = valid_ref[mine + a]


def edge(shape, start, count, key):
    row = lax.broadcasted_iota(jnp.int32, shape, 0) + start
    lane = lax.broadcasted_iota(jnp.int32, shape, 1)
    mine, other = (0, 1) if key else (1, 0)
    return jnp.where(lane == mine, jnp.where(row < count, 0.0, -BIG), jnp.where(lane == other, 1.0, 0.0)).astype(jnp.bfloat16)


def nt(a, b):
    return lax.dot_general(a, b, (((1,), (1,)), ((), ())), preferred_element_type=F32)


def ceil_of(x, n):
    return (x + n - 1) // n


def stash(e, v, m, inside, outside, sems, out, skip=0):
    rows = pl.ds(0, m * UNIT)
    near, far = inside.at[e, pl.ds(0, v), rows], outside.at[e - skip, pl.ds(0, v), rows]
    return pltpu.make_async_copy(near, far, sems.at[e]) if out else pltpu.make_async_copy(far, near, sems.at[e])


def by_shape(keys, count, most, run):
    spans, units = ceil_of(keys, SPAN), ceil_of(count, UNIT)
    for v in range(1, most + 1):
        @pl.when(spans == v)
        def _():
            for m in range(1, most + 1):
                pl.when(units == m)(functools.partial(run, v, m))


def first_kernel(tiles, n_tm, dp_ref, slot_ref, valid_ref, order_ref, s_ref, every, sofar_ref, col_ref, row_ref, send_ref, own_ref, ok_ref, sum_ref, e_hbm,
                 s_buf, row_buf, t_buf, right, key_edge, key_full, acc, col, ends, e_buf, meta, sems, e_sems, out_sem, row_sem):
    me, tm = lax.axis_index("dp"), lax.axis_index("tm")
    frames, width = s_ref.shape[1], s_ref.shape[2]
    total = 2 * tiles
    spans_most = frames // SPAN
    scale = 1.0 / math.sqrt(width)
    c2 = scale / math.log(2.0)
    bring = pltpu.make_async_copy(s_ref, s_buf, out_sem)
    bring.start()
    lay_table(meta, tiles, me, tm, n_tm, dp_ref, slot_ref, valid_ref, order_ref)

    def fetch(e):
        return pltpu.make_async_copy(every.at[meta[0, e]], t_buf.at[e], sems.at[e])
    for e in range(STARTED, total):
        fetch(e).start()
    for a in range(2):
        right[a] = edge((frames, width), 0, meta[4, a], False)
    key_full[...] = edge((SPAN, width), 0, SPAN, True)
    ok_ref[0] = 1
    sum_ref[...] = jnp.zeros_like(sum_ref)
    ends[...] = jnp.ones_like(ends)
    lane = lax.broadcasted_iota(jnp.int32, (1, frames), 1)
    send_ref[...] = jnp.zeros_like(send_ref)

    def put(e, values):
        @pl.when(e < 2)
        def _():
            own_ref[e] = values

        @pl.when(e >= 2)
        def _():
            send_ref[meta[2, e]] = values

    def fold(sums):
        return jnp.concatenate([sums[:, r * 128:(r + 1) * 128] for r in range(frames // 128)], axis=0)

    frame = lax.broadcasted_iota(jnp.int32, (8, 128), 0) * 128 + lax.broadcasted_iota(jnp.int32, (8, 128), 1)

    def finish(e, sums):
        real = frame < meta[1, e]
        sums = jnp.where(real, sums, 1.0)
        ends[0] = jnp.minimum(ends[0], sums)
        ends[1] = jnp.maximum(ends[1], sums)
        put(e, jnp.where(real, jnp.log(sums), -BIG))

    def tile(e, carry):
        a = meta[3, e]
        keys = meta[1, e]
        fetch(e).wait()
        key_edge[...] = edge((SPAN, width), (ceil_of(keys, SPAN) - 1) * SPAN, keys, True)

        def run(v, m):
            n = UNIT * m
            lhs = jnp.concatenate([s_buf[a, :n, :], right[a, :n, :]], axis=1)
            part = acc[a, :n, :]
            for j in range(v):
                cols = slice(j * SPAN, (j + 1) * SPAN)
                side = key_edge if j == v - 1 else key_full
                rhs = jnp.concatenate([t_buf[e, cols, :], side[...]], axis=1)
                p = jnp.exp2(nt(lhs, rhs) * c2)
                e_buf[e - STARTED, j, :n, :] = p.astype(jnp.bfloat16)
                for w in range(SPAN // 128):
                    part = part + p[:, w * 128:(w + 1) * 128]
                col[:, cols] = jnp.sum(p.reshape(n // 8, 8, SPAN), axis=0)
            acc[a, :n, :] = part
            stash(e - STARTED, v, m, e_buf, e_hbm, e_sems, True).start()
        by_shape(keys, meta[4, e], spans_most, run)
        finish(e, fold(jnp.sum(col[...], axis=0, keepdims=True)))
        return carry

    sofar = pltpu.make_async_copy(sofar_ref, acc, row_sem)
    sofar.start()
    for e in range(STARTED):
        finish(e, col_ref[e])
    sofar.wait()
    bring.wait()
    lax.fori_loop(STARTED, total, tile, 0)

    low, high = jnp.min(ends[0]), jnp.max(ends[1])
    row = lax.broadcasted_iota(jnp.int32, (frames, 128), 0)
    for a in range(2):
        sums = jnp.broadcast_to(jnp.sum(acc[a], axis=1, keepdims=True), (frames, 128))
        sums = jnp.where(row < meta[4, a], sums, 1.0)
        low, high = jnp.minimum(low, jnp.min(sums)), jnp.maximum(high, jnp.max(sums))
        row_buf[a] = (0.5 * scale) / sums
        sum_ref[...] += jnp.sum(jnp.log(sums).reshape(frames // 8, 8, 128), axis=0)

    @pl.when(jnp.logical_not((low >= LOW) & (high <= HIGH)))
    def _():
        ok_ref[0] = 0
        row_buf[...] = jnp.full(row_buf.shape, -BIG, F32)
        acc[...] = jnp.zeros_like(acc)
        sum_ref[...] = jnp.zeros_like(sum_ref)
        half = 128
        for e in range(STARTED):
            fetch(e).start()
        for e in range(STARTED):
            fetch(e).wait()

        def slow_tile(e, carry):
            a = meta[3, e]
            keys = meta[1, e]
            col[0:1, :] = jnp.full((1, frames), -BIG, F32)
            col[1:2, :] = jnp.zeros((1, frames), F32)

            def slow_chunk(i, c):
                rows = pl.ds(pl.multiple_of(i * half, half), half)
                lhs = jnp.concatenate([s_buf[a, rows, :], right[a, rows, :]], axis=1)
                for j in range(frames // half):
                    cols = slice(j * half, (j + 1) * half)
                    rhs = jnp.concatenate([t_buf[e, cols, :], edge((half, width), j * half, keys, True)], axis=1)
                    sc = nt(lhs, rhs) * scale
                    old = row_buf[a, rows, :]
                    new = jnp.maximum(old, jnp.broadcast_to(jnp.max(sc, axis=1, keepdims=True), (half, 128)))
                    acc[a, rows, :] = acc[a, rows, :] * jnp.exp(old - new) + jnp.broadcast_to(
                        jnp.sum(jnp.where(sc > -0.01 * BIG, jnp.exp(sc - new[:, :1]), 0.0), axis=1, keepdims=True), (half, 128))
                    row_buf[a, rows, :] = new
                    cold = col[0:1, cols]
                    cnew = jnp.maximum(cold, jnp.max(sc, axis=0, keepdims=True))
                    col[1:2, cols] = col[1:2, cols] * jnp.exp(cold - cnew) + jnp.sum(
                        jnp.where(sc > -0.01 * BIG, jnp.exp(sc - cnew), 0.0), axis=0, keepdims=True)
                    col[0:1, cols] = cnew
                return c
            lax.fori_loop(0, frames // half, slow_chunk, 0)
            real = lane < keys
            put(e, fold(jnp.where(real, col[0:1, :] + jnp.log(jnp.where(real, col[1:2, :], 1.0)), -BIG)))
            return carry
        lax.fori_loop(0, total, slow_tile, 0)
        for a in range(2):
            lse = jnp.where(row < meta[4, a], row_buf[a] + jnp.log(jnp.maximum(acc[a], 1e-30)), 0.0)
            row_buf[a] = lse
            sum_ref[...] += jnp.sum(lse.reshape(frames // 8, 8, 128), axis=0)

    sum_ref[...] = sum_ref[...] * (1.0 / 128)

    give = pltpu.make_async_copy(row_buf, row_ref, out_sem)
    give.start()

    def drain(e, carry):
        by_shape(meta[1, e], meta[4, e], spans_most, lambda v, m: stash(e - STARTED, v, m, e_buf, e_hbm, e_sems, True).wait())
        return carry
    lax.fori_loop(STARTED, total, drain, 0)
    give.wait()


def first_pass(tables, student, every, sofar, cols, n_dp, n_tm, tiles):
    blocks, frames, width = student.shape
    total = blocks * tiles
    smem, vmem, far = (pl.BlockSpec(memory_space=m) for m in (pltpu.SMEM, pltpu.VMEM, pl.ANY))
    return pl.pallas_call(
        functools.partial(first_kernel, tiles, n_tm),
        out_shape=(
            jax.ShapeDtypeStruct((blocks, frames, 128), F32),
            jax.ShapeDtypeStruct((n_dp, 8, 128), F32),
            jax.ShapeDtypeStruct((blocks, 8, 128), F32),
            jax.ShapeDtypeStruct((1,), jnp.int32),
            jax.ShapeDtypeStruct((8, 128), F32),
            jax.ShapeDtypeStruct((total - STARTED, frames // SPAN, frames, SPAN), jnp.bfloat16),
        ),
        in_specs=[smem, smem, smem, smem, far, far, far, vmem],
        out_specs=(far, vmem, vmem, smem, vmem, far),
        scratch_shapes=[
            pltpu.VMEM((blocks, frames, width), jnp.bfloat16),
            pltpu.VMEM((blocks, frames, 128), F32),
            pltpu.VMEM((total, frames, width), jnp.bfloat16),
            pltpu.VMEM((blocks, frames, width), jnp.bfloat16),
            pltpu.VMEM((SPAN, width), jnp.bfloat16),
            pltpu.VMEM((SPAN, width), jnp.bfloat16),
            pltpu.VMEM((blocks, frames, 128), F32),
            pltpu.VMEM((8, frames), F32),
            pltpu.VMEM((2, 8, 128), F32),
            pltpu.VMEM((total - STARTED, frames // SPAN, frames, SPAN), jnp.bfloat16),
            pltpu.SMEM((5, total), jnp.int32),
            pltpu.SemaphoreType.DMA((total,)),
            pltpu.SemaphoreType.DMA((total - STARTED,)),
            pltpu.SemaphoreType.DMA,
            pltpu.SemaphoreType.DMA,
        ],
        compiler_params=pltpu.CompilerParams(vmem_limit_bytes=60 * 1024 * 1024),
        name="first_pass",
    )(*tables, student, every, sofar, cols)


def second_kernel(tiles, n_tm, dp_ref, slot_ref, valid_ref, order_ref, ok_ref, s_ref, every, e_first, e_then, row_ref, far_ref, own_ref, out_ref,
                  s_buf, row_buf, w_buf, acc, e_buf, meta, sems, e_sems, row_sem, s_sem):
    me, tm = lax.axis_index("dp"), lax.axis_index("tm")
    frames, width = s_ref.shape[1], s_ref.shape[2]
    total = 2 * tiles
    spans_most = frames // SPAN
    scale = 1.0 / math.sqrt(width)
    lay_table(meta, tiles, me, tm, n_tm, dp_ref, slot_ref, valid_ref, order_ref)

    def fetch(e):
        return pltpu.make_async_copy(every.at[meta[0, e]], w_buf.at[e, :, pl.ds(0, width)], sems.at[e])

    def loader(store, skip):
        def load(e, carry):
            fetch(e).start()

            @pl.when(ok_ref[0] != 0)
            def _():
                by_shape(meta[1, e], meta[4, e], spans_most,
                         lambda v, m: stash(e, v, m, e_buf, store, e_sems, False, skip).start())
            return carry
        return load
    lax.fori_loop(0, STARTED, loader(e_first, 0), 0)
    lax.fori_loop(STARTED, total, loader(e_then, STARTED), 0)
    rows_in = pltpu.make_async_copy(row_ref, row_buf, row_sem)
    rows_in.start()
    acc[...] = jnp.zeros_like(acc)

    def lse_row(e, r):
        return jnp.where(e < 2, own_ref[meta[3, e], r:r + 1, :], far_ref[meta[2, e], r:r + 1, :])

    def tile(e, carry):
        a = meta[3, e]
        fetch(e).wait()

        def run(v, m):
            n = UNIT * m
            for r in range(v * SPAN // 128):
                rows = slice(r * 128, (r + 1) * 128)
                weight = jnp.broadcast_to((0.5 * scale) * jnp.exp(-lse_row(e, r)), (128, 128)).T
                w_buf[e, rows, width:] = (weight * w_buf[e, rows, :width].astype(F32)).astype(w_buf.dtype)
            stash(e, v, m, e_buf, e_first, e_sems, False, e).wait()
            lhs = jnp.concatenate([e_buf[e, j, :n, :] for j in range(v)], axis=1)
            acc[a, :n, :] += jnp.dot(lhs, w_buf[e, :v * SPAN, :], preferred_element_type=F32)
        by_shape(meta[1, e], meta[4, e], spans_most, run)
        return carry

    @pl.when(ok_ref[0] != 0)
    def _():
        lax.fori_loop(0, total, tile, 0)

    @pl.when(ok_ref[0] == 0)
    def _():
        half = 128
        students = pltpu.make_async_copy(s_ref, s_buf, s_sem)
        students.start()
        students.wait()

        def slow_tile(e, carry):
            a = meta[3, e]
            fetch(e).wait()

            def slow_chunk(i, c):
                rows = pl.ds(pl.multiple_of(i * half, half), half)
                part = acc[a, rows, width:]
                for j in range(frames // half):
                    t = w_buf[e, j * half:(j + 1) * half, :width]
                    inside = lax.broadcasted_iota(jnp.int32, (half, half), 1) + j * half < meta[1, e]
                    sc = nt(s_buf[a, rows, :], t) * scale
                    g = 0.5 * (jnp.exp(jnp.where(inside, sc - row_buf[a, rows, :], -BIG))
                               + jnp.exp(jnp.where(inside, sc - lse_row(e, j), -BIG)))
                    part = part + scale * jnp.dot(g.astype(jnp.bfloat16), t, preferred_element_type=F32)
                acc[a, rows, width:] = part
                return c
            lax.fori_loop(0, ceil_of(meta[4, e], half), slow_chunk, 0)
            return carry
        lax.fori_loop(0, total, slow_tile, 0)
        acc[:, :, :width] = jnp.zeros_like(acc[:, :, :width])

    rows_in.wait()
    row = lax.broadcasted_iota(jnp.int32, (frames, width), 0)
    for a in range(2):
        grad = row_buf[a] * acc[a, :, :width] + acc[a, :, width:] - scale * w_buf[a, :, :width].astype(F32)
        out_ref[a] = jnp.where(row < meta[4, a], grad, 0.0).astype(out_ref.dtype)


def second_pass(tables, ok, student, every, begun, kept, rows, far, own, n_tm, tiles):
    blocks, frames, width = student.shape
    total = blocks * tiles
    smem, vmem, hbm = (pl.BlockSpec(memory_space=m) for m in (pltpu.SMEM, pltpu.VMEM, pl.ANY))
    return pl.pallas_call(
        functools.partial(second_kernel, tiles, n_tm),
        out_shape=jax.ShapeDtypeStruct(student.shape, student.dtype),
        in_specs=[smem, smem, smem, smem, smem, hbm, hbm, hbm, hbm, hbm, vmem, vmem],
        out_specs=vmem,
        scratch_shapes=[
            pltpu.VMEM((blocks, frames, width), jnp.bfloat16),
            pltpu.VMEM((blocks, frames, 128), F32),
            pltpu.VMEM((total, frames, 2 * width), jnp.bfloat16),
            pltpu.VMEM((blocks, frames, 2 * width), F32),
            pltpu.VMEM((total, frames // SPAN, frames, SPAN), jnp.bfloat16),
            pltpu.SMEM((5, total), jnp.int32),
            pltpu.SemaphoreType.DMA((total,)),
            pltpu.SemaphoreType.DMA((total,)),
            pltpu.SemaphoreType.DMA,
            pltpu.SemaphoreType.DMA,
        ],
        compiler_params=pltpu.CompilerParams(vmem_limit_bytes=60 * 1024 * 1024),
        name="second_pass",
    )(*tables, ok, student, every, begun, kept, rows, far, own)


def exchange_kernel(n_dp, n_tm, valid_ref, ask_ref, side_ref, send_ref, own_ref, sum_ref, far_ref, lse_ref, loss_ref,
                    inc, reply, across, column, s1, r1, s2, r2, s3, r3, s4, r4):
    me, tm = lax.axis_index("dp"), lax.axis_index("tm")
    others = [(me + o) % n_dp for o in range(1, n_dp)]
    beside = [(tm + o) % n_tm for o in range(1, n_tm)]
    barrier = pltpu.get_barrier_semaphore()
    for to in others:
        pl.semaphore_signal(barrier, inc=1, device_id=(to, tm), device_id_type=MESH)
    for to in beside:
        pl.semaphore_signal(barrier, inc=1, device_id=(me, to), device_id_type=MESH)
    inc[me] = send_ref[me]
    pl.semaphore_wait(barrier, n_dp - 1 + n_tm - 1)

    def ship(src, dst, sent, got, where):
        pltpu.make_async_remote_copy(
            src_ref=src, dst_ref=dst, send_sem=sent, recv_sem=got, device_id=where, device_id_type=MESH).start()

    for to in others:
        ship(send_ref.at[to], inc.at[me], s1, r1, (to, tm))
    settle(inc, r1, n_dp - 1)
    terms = sum_ref[...] + side_ref[0]
    frame = lax.broadcasted_iota(jnp.int32, (8, 128), 0) * 128 + lax.broadcasted_iota(jnp.int32, (8, 128), 1)
    for a in range(2):
        best = own_ref[a]
        for p in range(n_dp):
            best = jnp.maximum(best, inc[p] + ask_ref[p, a])
        total = jnp.exp(own_ref[a] - best)
        for p in range(n_dp):
            total = total + jnp.exp(inc[p] + ask_ref[p, a] - best)
        lse = jnp.where(frame < valid_ref[(me * n_tm + tm) * 2 + a], best + jnp.log(total), 0.0)
        lse_ref[a] = lse
        terms = terms + lse
    across[tm] = terms
    for p in range(n_dp):
        share = ask_ref[p, 2]
        reply[p] = lse_ref[0] * (1.0 - share) + lse_ref[1] * share
    far_ref[me] = reply[me]
    for to in beside:
        ship(across.at[tm], across.at[tm], s3, r3, (me, to))
    for to in others:
        ship(reply.at[to], far_ref.at[me], s2, r2, (to, tm))
    settle(across, r3, n_tm - 1)
    rows = across[0]
    for t in range(1, n_tm):
        rows = rows + across[t]
    column[me] = rows
    for to in others:
        ship(column.at[me], column.at[me], s4, r4, (to, tm))
    settle(far_ref, r2, n_dp - 1)
    settle(column, r4, n_dp - 1)
    rows = column[0]
    for p in range(1, n_dp):
        rows = rows + column[p]
    loss_ref[0] = jnp.sum(rows * side_ref[1])
    settle(send_ref, s1, n_dp - 1)
    settle(reply, s2, n_dp - 1)
    settle(across, s3, n_tm - 1)
    settle(column, s4, n_dp - 1)


def exchange(valid, ask, side, send, own, sums, n_tm):
    n_dp = send.shape[0]
    smem, vmem = pl.BlockSpec(memory_space=pltpu.SMEM), pl.BlockSpec(memory_space=pltpu.VMEM)
    return pl.pallas_call(
        functools.partial(exchange_kernel, n_dp, n_tm),
        out_shape=(
            jax.ShapeDtypeStruct((n_dp, 8, 128), F32),
            jax.ShapeDtypeStruct((2, 8, 128), F32),
            jax.ShapeDtypeStruct((1,), F32),
        ),
        in_specs=[smem] + [vmem] * 5,
        out_specs=(vmem, vmem, smem),
        scratch_shapes=[
            pltpu.VMEM((n_dp, 8, 128), F32), pltpu.VMEM((n_dp, 8, 128), F32),
            pltpu.VMEM((n_tm, 8, 128), F32), pltpu.VMEM((n_dp, 8, 128), F32),
        ] + [pltpu.SemaphoreType.DMA] * 8,
        compiler_params=pltpu.CompilerParams(collective_id=1, has_side_effects=True),
        name="exchange",
    )(valid, ask, side, send, own, sums)


def body(student, teacher, partner_dp, partner_slot, valid_frames):
    n_dp, n_tm = lax.axis_size("dp"), lax.axis_size("tm")
    blocks, frames, width = student.shape
    tiles = partner_dp.shape[1] + 1
    tables = (partner_dp.T, partner_slot.T, valid_frames)
    every, begun, sofar, ask, side, order, cols = gather(teacher, student, tables, n_dp, n_tm)
    every = every.reshape(n_dp * blocks, frames, width)
    tables = tables + (order,)
    rows, send, own, ok, sums, kept = first_pass(tables, student, every, sofar, cols, n_dp, n_tm, tiles)
    far, lse, loss = exchange(valid_frames, ask, side, send, own, sums, n_tm)
    grad = second_pass(tables, ok, student, every, begun, kept, rows, far, lse, n_tm, tiles)
    return (loss[0], grad)


def solution(mesh):
    placed = (P(("dp", "tm"), None, None), P(("dp", "tm"), None, None), P(), P(), P())
    return jax.shard_map(
        body,
        mesh=mesh,
        in_specs=placed,
        out_specs=(P(), P(("dp", "tm"), None, None)),
        check_vma=False,
    )
```

```python
import functools
import heapq
import math

import jax
import jax.numpy as jnp
from jax import lax
from jax.experimental import pallas as pl
from jax.experimental.pallas import tpu as pltpu
from jax.sharding import PartitionSpec as P

MESH = pl.DeviceIdType.MESH
F32 = jnp.float32
BIG = 1e30

PARTS = 2
ZP, ZM, YP, YM = range(4)
MOVE = {ZP: (1, 0), ZM: (-1, 0), YP: (0, 1), YM: (0, -1)}
FIRST = ((0, 0), (0, 1), (0, 3), (1, 0), (3, 0), (2, 0), (1, 1), (3, 1), (0, 2), (1, 3), (3, 3))
NEXT = ((2, 1), (2, 3))
LAST = ((1, 2), (3, 2), (2, 2))
CHIPS = FIRST + NEXT + LAST
EARLY = 10
SURE = 6
STARTED = 2 + EARLY


def onward(tile, oz, oy, part):
    half = part * 2 // PARTS
    first, second = (oz, oy) if tile == 0 else (oy, oz)
    plus1, minus1 = (ZP, ZM) if tile == 0 else (YP, YM)
    plus2, minus2 = (YP, YM) if tile == 0 else (ZP, ZM)
    links = []
    if second == 0:
        if first == 0:
            links += [plus1, minus1]
        elif first == 1 and half == 0:
            links += [plus1]
        elif first == 3 and half == 1:
            links += [minus1]
        links += [plus2, minus2]
    elif second == 1 and half == 0:
        links += [plus2]
    elif second == 3 and half == 1:
        links += [minus2]
    return links


def moved(oz, oy, link):
    dz, dy = MOVE[link]
    return (oz + dz) % 4, (oy + dy) % 4


def plan():
    free = [0.0] * 4
    events, order, count = [], [], 0

    def send(unit, link, now):
        nonlocal count
        tile, oz, oy, part = unit
        free[link] = max(now, free[link]) + 1.0
        noz, noy = moved(oz, oy, link)
        heapq.heappush(events, (free[link] + 0.5, count, (tile, noz, noy, part), link))
        count += 1

    first = []
    for link in range(4):
        near = 0 if link in (ZP, ZM) else 1
        lead = 0 if link in (ZP, YP) else 1
        for tile in (near, 1 - near):
            for part in range(PARTS):
                first.append(((tile, 0, 0, part if lead == 0 else PARTS - 1 - part), link))
    first = [first[k * 2 * PARTS + i] for i in range(2 * PARTS) for k in range(4)]
    for unit, link in first:
        send(unit, link, 0.0)
    while events:
        now, _, unit, _ = heapq.heappop(events)
        out = onward(*unit)
        order.append((unit, out))
        for link in out:
            send(unit, link, now)
    return first, order


def lay_requests(me, tm, n_tm, dp_ref, slot_ref, ask_ref):
    asked = jnp.max(jnp.where(dp_ref[...] == me, slot_ref[...], -1).astype(F32), axis=0, keepdims=True)
    lane = lax.broadcasted_iota(jnp.int32, asked.shape, 1) // 2
    for p in range(ask_ref.shape[0]):
        one = jnp.max(jnp.where(lane == p * n_tm + tm, asked, -1.0), axis=1, keepdims=True)
        one = jnp.broadcast_to(one, (8, 128))
        ask_ref[p, 0] = jnp.where(one == 0.0, 0.0, -BIG)
        ask_ref[p, 1] = jnp.where(one == 1.0, 0.0, -BIG)
        ask_ref[p, 2] = jnp.maximum(one, 0.0)


def lay_side(me, tm, n_tm, t_ref, s_ref, valid_ref, side_ref):
    blocks, frames, width = t_ref.shape
    row = lax.broadcasted_iota(jnp.int32, (frames, width), 0)
    total = jnp.zeros((8, width), F32)
    for a in range(blocks):
        both = s_ref[a].astype(F32) * t_ref[a].astype(F32)
        both = jnp.where(row < valid_ref[(me * n_tm + tm) * blocks + a], both, 0.0)
        total = total + jnp.sum(both.reshape(frames // 8, 8, width), axis=0)
    side_ref[0] = total * (-2.0 / math.sqrt(width))
    count = lax.fori_loop(0, valid_ref.shape[0], lambda i, c: c + valid_ref[i], jnp.int32(0))
    side_ref[1] = 0.5 / jnp.full((8, width), count).astype(F32)


def settle(buf, sem, count):
    part = buf.at[pl.ds(0, count)]
    pltpu.make_async_copy(part, part, sem).wait()


def gather_kernel(n_tm, t_ref, s_ref, dpv_ref, slotv_ref, dp_ref, slot_ref, valid_ref,
                  out_ref, e_hbm, acc_hbm, ask_hbm, side_ref, order_ref, col_ref,
                  first_buf, next_buf, e_buf, acc, right, ask, found_at, rank_at,
                  send_sem, recv_sem, peer_send, peer_recv, own_sem, out_sem, e_sem, more_sem):
    frames, width = t_ref.shape[1], t_ref.shape[2]
    n = frames // PARTS
    me, tm = lax.axis_index("dp"), lax.axis_index("tm")
    z, y, c = me // 8, (me // 2) % 4, me % 2
    c2 = 1.0 / math.sqrt(width) / math.log(2.0)

    def dp_of(zz, yy, cc):
        return (zz * 4 + yy) * 2 + cc

    def device_of(oz, oy, cc):
        return dp_of((z + 4 - oz) % 4, (y + 4 - oy) % 4, cc)

    near = [
        dp_of((z + 1) % 4, y, c), dp_of((z + 3) % 4, y, c),
        dp_of(z, (y + 1) % 4, c), dp_of(z, (y + 3) % 4, c),
    ]
    peer = dp_of(z, y, 1 - c)
    barrier = pltpu.get_barrier_semaphore()
    for other in near + [peer]:
        pl.semaphore_signal(barrier, inc=1, device_id=(other, tm), device_id_type=MESH)
    pl.semaphore_wait(barrier, 5)

    def recv_id(unit):
        tile, oz, oy, part = unit
        return ((tile * 4 + oz) * 4 + oy) * PARTS + part

    def device_store(oz, oy, cc):
        if (oz, oy) in FIRST:
            return first_buf.at[FIRST.index((oz, oy)) * 2 + cc]
        if (oz, oy) in NEXT:
            return next_buf.at[NEXT.index((oz, oy)) * 2 + cc]
        return out_ref.at[device_of(oz, oy, cc)]

    def place(unit):
        tile, oz, oy, part = unit
        return device_store(oz, oy, c).at[tile, pl.ds(part * n, n)]

    def source(unit):
        tile, oz, oy, part = unit
        return t_ref.at[tile, pl.ds(part * n, n)] if (oz, oy) == (0, 0) else place(unit)

    def onto(unit, link):
        tile, oz, oy, part = unit
        noz, noy = moved(oz, oy, link)
        if (noz, noy) in LAST:
            return out_ref.at[device_of(oz, oy, c), tile, pl.ds(part * n, n)]
        return place((tile, noz, noy, part))

    def send(unit, link):
        tile, oz, oy, part = unit
        pltpu.make_async_remote_copy(
            src_ref=source(unit), dst_ref=onto(unit, link),
            send_sem=send_sem, recv_sem=recv_sem.at[recv_id((tile, *moved(oz, oy, link), part))],
            device_id=(near[link], tm), device_id_type=MESH,
        ).start()

    def group(oz, oy):
        return 0 if (oz, oy) in FIRST else 1 if (oz, oy) in NEXT else 2

    def share(unit):
        pltpu.make_async_remote_copy(
            src_ref=source(unit), dst_ref=place(unit),
            send_sem=peer_send, recv_sem=peer_recv.at[group(unit[1], unit[2])],
            device_id=(peer, tm), device_id_type=MESH,
        ).start()

    def keep(oz, oy, cc):
        pltpu.make_async_copy(device_store(oz, oy, cc), out_ref.at[device_of(oz, oy, cc)], out_sem).start()

    first, order = plan()
    for unit, link in first:
        send(unit, link)
    for tile in (0, 1):
        for part in range(PARTS):
            share((tile, 0, 0, part))
    own = pltpu.make_async_copy(t_ref, device_store(0, 0, c), own_sem)
    own.start()
    pltpu.make_async_copy(t_ref, out_ref.at[me], out_sem).start()

    mine = (me * n_tm + tm) * 2
    partners = dp_ref.shape[0]

    def lay_order():
        names = [dp_ref[k, mine + a] for a in range(2) for k in range(partners)]
        rank = jnp.int32(0)
        for q in range(2 * len(CHIPS)):
            p = device_of(*CHIPS[q // 2], q % 2)
            found = jnp.int32(0)
            for j, name in enumerate(names):
                found = jnp.where(name == p, j + 1, found)
            found_at[q] = found
            rank_at[q] = jnp.where(found > 0, rank, -1)
            rank = rank + jnp.where(found > 0, 1, 0)
        where_ = []
        for r in range(2 * partners):
            at, entry = jnp.int32(0), jnp.int32(0)
            for q in range(r, r + 2 * partners + 1):
                if q < 2 * len(CHIPS):
                    hit = rank_at[q] == r
                    at = jnp.where(hit, q, at)
                    entry = jnp.where(hit, found_at[q] - 1, entry)
            order_ref[r] = entry
            where_.append(at)
        return where_

    def score(pos, a, keys, load, own_block):
        lhs = jnp.concatenate([s_ref[a], right[a]], axis=1)
        part = jnp.zeros((frames, 128), F32)
        for j in range(frames // SPAN):
            rhs = jnp.concatenate([load(slice(j * SPAN, (j + 1) * SPAN)), edge((SPAN, width), j * SPAN, keys, True)], axis=1)
            p = jnp.exp2(nt(lhs, rhs) * c2)
            e_buf[pos, j] = p.astype(jnp.bfloat16)
            for w in range(SPAN // 128):
                part = part + p[:, w * 128:(w + 1) * 128]
            sums = jnp.sum(p, axis=0, keepdims=True)
            for w in range(SPAN // 128):
                r = j * (SPAN // 128) + w
                col_ref[pos, r:r + 1, :] = sums[:, w * 128:(w + 1) * 128]
        if own_block:
            acc[a] = part
        else:
            for b in range(2):
                acc[b] += jnp.where(a == b, part, 0.0)
        pltpu.make_async_copy(e_buf.at[pos], e_hbm.at[pos], e_sem).start()

    def score_own(a):
        score(a, a, valid_ref[mine + a], lambda rows: t_ref[a, rows, :], True)

    def score_early(r, at):
        entry = order_ref[r]
        a, k = entry // partners, entry % partners
        slot = slot_ref[k, mine + a]
        keys = valid_ref[(dp_ref[k, mine + a] * n_tm + tm) * 2 + slot]
        many = 2 * len(FIRST)

        def load(rows):
            block = first_buf[jnp.minimum(at, many - 1), slot, rows, :]
            if r < SURE:
                return block
            later = next_buf[jnp.clip(at - many, 0, 2 * len(NEXT) - 1), slot, rows, :]
            return jnp.where(at < many, block, later)
        score(2 + r, a, keys, load, False)

    right[0] = edge((frames, width), 0, valid_ref[mine], False)
    right[1] = edge((frames, width), 0, valid_ref[mine + 1], False)
    lay_requests(me, tm, n_tm, dpv_ref, slotv_ref, ask)
    asks = pltpu.make_async_copy(ask, ask_hbm, more_sem.at[0])
    asks.start()
    at = lay_order()
    spots = [unit[1:3] for unit, _ in order]
    first_done = max(i for i, s in enumerate(spots) if s in FIRST)
    next_done = max(i for i, s in enumerate(spots) if s in NEXT)
    work = {4: lambda: lay_side(me, tm, n_tm, t_ref, s_ref, valid_ref, side_ref),
            6: lambda: score_own(0), 12: lambda: score_own(1)}
    missing = {chip: 2 * PARTS for chip in CHIPS}
    waiting = []
    for i, (unit, out) in enumerate(order):
        here = place(unit)
        pltpu.make_async_remote_copy(
            src_ref=here, dst_ref=here, send_sem=send_sem, recv_sem=recv_sem.at[recv_id(unit)],
            device_id=(near[0], tm), device_id_type=MESH,
        ).wait_recv()
        for link in out:
            send(unit, link)
        share(unit)
        chip = unit[1:3]
        missing[chip] -= 1
        if missing[chip] == 0 and chip not in LAST:
            keep(*chip, c)
        if i in work:
            work[i]()
        if i == first_done + 1:
            own.wait()
            settle(first_buf, peer_recv.at[0], len(FIRST))
            for chip in FIRST:
                keep(*chip, 1 - c)
            waiting += list(range(SURE))
        if i == next_done + 1:
            settle(next_buf, peer_recv.at[1], len(NEXT))
            for chip in NEXT:
                keep(*chip, 1 - c)
            waiting += list(range(SURE, EARLY))
        if waiting:
            r = waiting.pop(0)
            score_early(r, at[r])
    for r in waiting:
        score_early(r, at[r])
    sums = pltpu.make_async_copy(acc, acc_hbm, more_sem.at[1])
    sums.start()
    settle(out_ref, peer_recv.at[2], len(LAST))
    settle(out_ref, peer_send, len(CHIPS))
    settle(out_ref, send_sem, len(CHIPS) - 1)
    settle(out_ref, out_sem, 2 * (len(FIRST) + len(NEXT)))
    settle(e_hbm, e_sem, STARTED)
    asks.wait()
    sums.wait()


def gather(teacher, student, tables, n_dp, n_tm):
    blocks, frames, width = teacher.shape
    smem, vmem, far = (pl.BlockSpec(memory_space=m) for m in (pltpu.SMEM, pltpu.VMEM, pl.ANY))
    kept = (STARTED, frames // SPAN, frames, SPAN)
    dma = pltpu.SemaphoreType.DMA
    return pl.pallas_call(
        functools.partial(gather_kernel, n_tm),
        out_shape=(
            jax.ShapeDtypeStruct((n_dp, blocks, frames, width), teacher.dtype),
            jax.ShapeDtypeStruct(kept, jnp.bfloat16),
            jax.ShapeDtypeStruct((blocks, frames, 128), F32),
            jax.ShapeDtypeStruct((n_dp, 3, 8, 128), F32),
            jax.ShapeDtypeStruct((2, 8, 128), F32),
            jax.ShapeDtypeStruct((blocks * tables[0].shape[0],), jnp.int32),
            jax.ShapeDtypeStruct((STARTED, 8, 128), F32),
        ),
        in_specs=[vmem, vmem, vmem, vmem, smem, smem, smem],
        out_specs=(far, far, far, far, vmem, smem, vmem),
        scratch_shapes=[
            pltpu.VMEM((2 * len(FIRST), blocks, frames, width), teacher.dtype),
            pltpu.VMEM((2 * len(NEXT), blocks, frames, width), teacher.dtype),
            pltpu.VMEM(kept, jnp.bfloat16),
            pltpu.VMEM((blocks, frames, 128), F32),
            pltpu.VMEM((blocks, frames, width), jnp.bfloat16),
            pltpu.VMEM((n_dp, 3, 8, 128), F32),
            pltpu.SMEM((2 * len(CHIPS),), jnp.int32),
            pltpu.SMEM((2 * len(CHIPS),), jnp.int32),
            dma, dma((32 * PARTS,)), dma, dma((3,)), dma, dma, dma, dma((2,)),
        ],
        compiler_params=pltpu.CompilerParams(
            collective_id=0, has_side_effects=True, vmem_limit_bytes=60 * 1024 * 1024),
        name="gather",
    )(teacher, student, tables[0], tables[1], *tables)


LOW, HIGH = 2.0 ** -60, 2.0 ** 100
SPAN = 256
UNIT = 256


def lay_table(meta, tiles, me, tm, n_tm, dp_ref, slot_ref, valid_ref, order_ref):
    mine = (me * n_tm + tm) * 2
    for e in range(2 * tiles):
        if e < 2:
            a, far, slot = e, me, e
        else:
            entry = order_ref[e - 2]
            a, k = entry // (tiles - 1), entry % (tiles - 1)
            far, slot = dp_ref[k, mine + a], slot_ref[k, mine + a]
        meta[0, e] = far * 2 + slot
        meta[1, e] = valid_ref[(far * n_tm + tm) * 2 + slot]
        meta[2, e] = far
        meta[3, e] = a
        meta[4, e] = valid_ref[mine + a]


def edge(shape, start, count, key):
    row = lax.broadcasted_iota(jnp.int32, shape, 0) + start
    lane = lax.broadcasted_iota(jnp.int32, shape, 1)
    mine, other = (0, 1) if key else (1, 0)
    return jnp.where(lane == mine, jnp.where(row < count, 0.0, -BIG), jnp.where(lane == other, 1.0, 0.0)).astype(jnp.bfloat16)


def nt(a, b):
    return lax.dot_general(a, b, (((1,), (1,)), ((), ())), preferred_element_type=F32)


def ceil_of(x, n):
    return (x + n - 1) // n


def stash(e, v, m, inside, outside, sems, out, skip=0):
    rows = pl.ds(0, m * UNIT)
    near, far = inside.at[e, pl.ds(0, v), rows], outside.at[e - skip, pl.ds(0, v), rows]
    return pltpu.make_async_copy(near, far, sems.at[e]) if out else pltpu.make_async_copy(far, near, sems.at[e])


def by_shape(keys, count, most, run, least=1):
    spans, units = ceil_of(keys, SPAN), jnp.maximum(ceil_of(count, UNIT), least)
    for v in range(1, most + 1):
        @pl.when(spans == v)
        def _():
            for m in range(least, most + 1):
                pl.when(units == m)(functools.partial(run, v, m))


def first_kernel(tiles, n_tm, dp_ref, slot_ref, valid_ref, order_ref, s_ref, every, sofar_ref, col_ref, row_ref, send_ref, own_ref, ok_ref, sum_ref, e_hbm,
                 s_buf, row_buf, t_buf, right, key_edge, key_full, acc, col, ends, e_buf, meta, sems, e_sems, out_sem, row_sem):
    me, tm = lax.axis_index("dp"), lax.axis_index("tm")
    frames, width = s_ref.shape[1], s_ref.shape[2]
    total = 2 * tiles
    spans_most = frames // SPAN
    scale = 1.0 / math.sqrt(width)
    c2 = scale / math.log(2.0)
    bring = pltpu.make_async_copy(s_ref, s_buf, out_sem)
    bring.start()
    lay_table(meta, tiles, me, tm, n_tm, dp_ref, slot_ref, valid_ref, order_ref)

    def fetch(e):
        return pltpu.make_async_copy(every.at[meta[0, e]], t_buf.at[e], sems.at[e])
    for e in range(STARTED, total):
        fetch(e).start()
    for a in range(2):
        right[a] = edge((frames, width), 0, meta[4, a], False)
    key_full[...] = edge((SPAN, width), 0, SPAN, True)
    ok_ref[0] = 1
    sum_ref[...] = jnp.zeros_like(sum_ref)
    ends[...] = jnp.ones_like(ends)
    lane = lax.broadcasted_iota(jnp.int32, (1, frames), 1)
    send_ref[...] = jnp.zeros_like(send_ref)

    def put(e, values):
        @pl.when(e < 2)
        def _():
            own_ref[e] = values

        @pl.when(e >= 2)
        def _():
            send_ref[meta[2, e]] = values

    def fold(sums):
        return jnp.concatenate([sums[:, r * 128:(r + 1) * 128] for r in range(frames // 128)], axis=0)

    frame = lax.broadcasted_iota(jnp.int32, (8, 128), 0) * 128 + lax.broadcasted_iota(jnp.int32, (8, 128), 1)

    def finish(e, sums):
        real = frame < meta[1, e]
        sums = jnp.where(real, sums, 1.0)
        ends[0] = jnp.minimum(ends[0], sums)
        ends[1] = jnp.maximum(ends[1], sums)
        put(e, jnp.where(real, jnp.log(sums), -BIG))

    def tile(e, carry):
        a = meta[3, e]
        keys = meta[1, e]
        fetch(e).wait()
        key_edge[...] = edge((SPAN, width), (ceil_of(keys, SPAN) - 1) * SPAN, keys, True)

        def run(v, m):
            n = UNIT * m
            lhs = jnp.concatenate([s_buf[a, :n, :], right[a, :n, :]], axis=1)
            part = acc[a, :n, :]
            for j in range(v):
                cols = slice(j * SPAN, (j + 1) * SPAN)
                side = key_edge if j == v - 1 else key_full
                rhs = jnp.concatenate([t_buf[e, cols, :], side[...]], axis=1)
                p = jnp.exp2(nt(lhs, rhs) * c2)
                e_buf[e - STARTED, j, :n, :] = p.astype(jnp.bfloat16)
                for w in range(SPAN // 128):
                    part = part + p[:, w * 128:(w + 1) * 128]
                col[:, cols] = jnp.sum(p.reshape(n // 8, 8, SPAN), axis=0)
            acc[a, :n, :] = part
            stash(e - STARTED, v, m, e_buf, e_hbm, e_sems, True).start()
        by_shape(keys, meta[4, e], spans_most, run)
        finish(e, fold(jnp.sum(col[...], axis=0, keepdims=True)))
        return carry

    sofar = pltpu.make_async_copy(sofar_ref, acc, row_sem)
    sofar.start()
    for e in range(STARTED):
        finish(e, col_ref[e])
    sofar.wait()
    bring.wait()
    lax.fori_loop(STARTED, total, tile, 0)

    low, high = jnp.min(ends[0]), jnp.max(ends[1])
    row = lax.broadcasted_iota(jnp.int32, (frames, 128), 0)
    for a in range(2):
        sums = jnp.broadcast_to(jnp.sum(acc[a], axis=1, keepdims=True), (frames, 128))
        sums = jnp.where(row < meta[4, a], sums, 1.0)
        low, high = jnp.minimum(low, jnp.min(sums)), jnp.maximum(high, jnp.max(sums))
        row_buf[a] = (0.5 * scale) / sums
        sum_ref[...] += jnp.sum(jnp.log(sums).reshape(frames // 8, 8, 128), axis=0)

    @pl.when(jnp.logical_not((low >= LOW) & (high <= HIGH)))
    def _():
        ok_ref[0] = 0
        row_buf[...] = jnp.full(row_buf.shape, -BIG, F32)
        acc[...] = jnp.zeros_like(acc)
        sum_ref[...] = jnp.zeros_like(sum_ref)
        half = 128
        for e in range(STARTED):
            fetch(e).start()
        for e in range(STARTED):
            fetch(e).wait()

        def slow_tile(e, carry):
            a = meta[3, e]
            keys = meta[1, e]
            col[0:1, :] = jnp.full((1, frames), -BIG, F32)
            col[1:2, :] = jnp.zeros((1, frames), F32)

            def slow_chunk(i, c):
                rows = pl.ds(pl.multiple_of(i * half, half), half)
                lhs = jnp.concatenate([s_buf[a, rows, :], right[a, rows, :]], axis=1)
                for j in range(frames // half):
                    cols = slice(j * half, (j + 1) * half)
                    rhs = jnp.concatenate([t_buf[e, cols, :], edge((half, width), j * half, keys, True)], axis=1)
                    sc = nt(lhs, rhs) * scale
                    old = row_buf[a, rows, :]
                    new = jnp.maximum(old, jnp.broadcast_to(jnp.max(sc, axis=1, keepdims=True), (half, 128)))
                    acc[a, rows, :] = acc[a, rows, :] * jnp.exp(old - new) + jnp.broadcast_to(
                        jnp.sum(jnp.where(sc > -0.01 * BIG, jnp.exp(sc - new[:, :1]), 0.0), axis=1, keepdims=True), (half, 128))
                    row_buf[a, rows, :] = new
                    cold = col[0:1, cols]
                    cnew = jnp.maximum(cold, jnp.max(sc, axis=0, keepdims=True))
                    col[1:2, cols] = col[1:2, cols] * jnp.exp(cold - cnew) + jnp.sum(
                        jnp.where(sc > -0.01 * BIG, jnp.exp(sc - cnew), 0.0), axis=0, keepdims=True)
                    col[0:1, cols] = cnew
                return c
            lax.fori_loop(0, frames // half, slow_chunk, 0)
            real = lane < keys
            put(e, fold(jnp.where(real, col[0:1, :] + jnp.log(jnp.where(real, col[1:2, :], 1.0)), -BIG)))
            return carry
        lax.fori_loop(0, total, slow_tile, 0)
        for a in range(2):
            lse = jnp.where(row < meta[4, a], row_buf[a] + jnp.log(jnp.maximum(acc[a], 1e-30)), 0.0)
            row_buf[a] = lse
            sum_ref[...] += jnp.sum(lse.reshape(frames // 8, 8, 128), axis=0)

    sum_ref[...] = sum_ref[...] * (1.0 / 128)

    give = pltpu.make_async_copy(row_buf, row_ref, out_sem)
    give.start()

    def drain(e, carry):
        by_shape(meta[1, e], meta[4, e], spans_most, lambda v, m: stash(e - STARTED, v, m, e_buf, e_hbm, e_sems, True).wait())
        return carry
    lax.fori_loop(STARTED, total, drain, 0)
    give.wait()


def first_pass(tables, student, every, sofar, cols, n_dp, n_tm, tiles):
    blocks, frames, width = student.shape
    total = blocks * tiles
    smem, vmem, far = (pl.BlockSpec(memory_space=m) for m in (pltpu.SMEM, pltpu.VMEM, pl.ANY))
    return pl.pallas_call(
        functools.partial(first_kernel, tiles, n_tm),
        out_shape=(
            jax.ShapeDtypeStruct((blocks, frames, 128), F32),
            jax.ShapeDtypeStruct((n_dp, 8, 128), F32),
            jax.ShapeDtypeStruct((blocks, 8, 128), F32),
            jax.ShapeDtypeStruct((1,), jnp.int32),
            jax.ShapeDtypeStruct((8, 128), F32),
            jax.ShapeDtypeStruct((total - STARTED, frames // SPAN, frames, SPAN), jnp.bfloat16),
        ),
        in_specs=[smem, smem, smem, smem, far, far, far, vmem],
        out_specs=(far, vmem, vmem, smem, vmem, far),
        scratch_shapes=[
            pltpu.VMEM((blocks, frames, width), jnp.bfloat16),
            pltpu.VMEM((blocks, frames, 128), F32),
            pltpu.VMEM((total, frames, width), jnp.bfloat16),
            pltpu.VMEM((blocks, frames, width), jnp.bfloat16),
            pltpu.VMEM((SPAN, width), jnp.bfloat16),
            pltpu.VMEM((SPAN, width), jnp.bfloat16),
            pltpu.VMEM((blocks, frames, 128), F32),
            pltpu.VMEM((8, frames), F32),
            pltpu.VMEM((2, 8, 128), F32),
            pltpu.VMEM((total - STARTED, frames // SPAN, frames, SPAN), jnp.bfloat16),
            pltpu.SMEM((5, total), jnp.int32),
            pltpu.SemaphoreType.DMA((total,)),
            pltpu.SemaphoreType.DMA((total - STARTED,)),
            pltpu.SemaphoreType.DMA,
            pltpu.SemaphoreType.DMA,
        ],
        compiler_params=pltpu.CompilerParams(vmem_limit_bytes=60 * 1024 * 1024),
        name="first_pass",
    )(*tables, student, every, sofar, cols)


def second_kernel(tiles, n_tm, dp_ref, slot_ref, valid_ref, order_ref, ok_ref, s_ref, every, e_first, e_then, row_ref, far_ref, own_ref, out_ref,
                  s_buf, row_buf, t_buf, w_even, w_odd, acc, e_buf, meta, sems, e_sems, row_sem, s_sem):
    me, tm = lax.axis_index("dp"), lax.axis_index("tm")
    frames, width = s_ref.shape[1], s_ref.shape[2]
    total = 2 * tiles
    spans_most = frames // SPAN
    scale = 1.0 / math.sqrt(width)
    lay_table(meta, tiles, me, tm, n_tm, dp_ref, slot_ref, valid_ref, order_ref)

    def fetch(e):
        return pltpu.make_async_copy(every.at[meta[0, e]], t_buf.at[e], sems.at[e])

    def loader(store, skip):
        def load(e, carry):
            fetch(e).start()

            @pl.when(ok_ref[0] != 0)
            def _():
                by_shape(meta[1, e], meta[4, e], spans_most,
                         lambda v, m: stash(e, v, m, e_buf, store, e_sems, False, skip).start(), 2)
            return carry
        return load
    lax.fori_loop(0, STARTED, loader(e_first, 0), 0)
    lax.fori_loop(STARTED, total, loader(e_then, STARTED), 0)
    rows_in = pltpu.make_async_copy(row_ref, row_buf, row_sem)
    rows_in.start()
    acc[...] = jnp.zeros_like(acc)

    def lse_row(e, r):
        return jnp.where(e < 2, own_ref[meta[3, e], r:r + 1, :], far_ref[meta[2, e], r:r + 1, :])

    def weigh(e, w_buf):
        for r in range(frames // 128):
            rows = slice(r * 128, (r + 1) * 128)
            weight = jnp.broadcast_to((0.5 * scale) * jnp.exp(-lse_row(e, r)), (128, 128)).T
            w_buf[rows, :] = (weight * t_buf[e, rows, :].astype(F32)).astype(w_buf.dtype)

    def tile(e, w_buf, w_next):
        a = meta[3, e]
        then = jnp.minimum(e + 1, total - 1)
        pl.when(e + 1 < total)(lambda: fetch(then).wait())

        def run(v, m):
            n = UNIT * m
            stash(e, v, m, e_buf, e_first, e_sems, False, e).wait()
            lhs = jnp.concatenate([e_buf[e, j, :n, :] for j in range(v)], axis=1)
            rhs = jnp.concatenate([t_buf[e, :v * SPAN, :], w_buf[:v * SPAN, :]], axis=1)
            acc[a, :n, :] += jnp.dot(lhs, rhs, preferred_element_type=F32)
            weigh(then, w_next)
        by_shape(meta[1, e], meta[4, e], spans_most, run, 2)

    @pl.when(ok_ref[0] != 0)
    def _():
        fetch(0).wait()
        weigh(0, w_even)

        def pair(i, carry):
            tile(2 * i, w_even, w_odd)
            tile(2 * i + 1, w_odd, w_even)
            return carry
        lax.fori_loop(0, total // 2, pair, 0)

    @pl.when(ok_ref[0] == 0)
    def _():
        half = 128
        students = pltpu.make_async_copy(s_ref, s_buf, s_sem)
        students.start()
        students.wait()

        def slow_tile(e, carry):
            a = meta[3, e]
            fetch(e).wait()

            def slow_chunk(i, c):
                rows = pl.ds(pl.multiple_of(i * half, half), half)
                part = acc[a, rows, width:]
                for j in range(frames // half):
                    t = t_buf[e, j * half:(j + 1) * half, :]
                    inside = lax.broadcasted_iota(jnp.int32, (half, half), 1) + j * half < meta[1, e]
                    sc = nt(s_buf[a, rows, :], t) * scale
                    g = 0.5 * (jnp.exp(jnp.where(inside, sc - row_buf[a, rows, :], -BIG))
                               + jnp.exp(jnp.where(inside, sc - lse_row(e, j), -BIG)))
                    part = part + scale * jnp.dot(g.astype(jnp.bfloat16), t, preferred_element_type=F32)
                acc[a, rows, width:] = part
                return c
            lax.fori_loop(0, ceil_of(meta[4, e], half), slow_chunk, 0)
            return carry
        lax.fori_loop(0, total, slow_tile, 0)
        acc[:, :, :width] = jnp.zeros_like(acc[:, :, :width])

    rows_in.wait()
    row = lax.broadcasted_iota(jnp.int32, (frames, width), 0)
    for a in range(2):
        grad = row_buf[a] * acc[a, :, :width] + acc[a, :, width:] - scale * t_buf[a].astype(F32)
        out_ref[a] = jnp.where(row < meta[4, a], grad, 0.0).astype(out_ref.dtype)


def second_pass(tables, ok, student, every, begun, kept, rows, far, own, n_tm, tiles):
    blocks, frames, width = student.shape
    total = blocks * tiles
    smem, vmem, hbm = (pl.BlockSpec(memory_space=m) for m in (pltpu.SMEM, pltpu.VMEM, pl.ANY))
    return pl.pallas_call(
        functools.partial(second_kernel, tiles, n_tm),
        out_shape=jax.ShapeDtypeStruct(student.shape, student.dtype),
        in_specs=[smem, smem, smem, smem, smem, hbm, hbm, hbm, hbm, hbm, vmem, vmem],
        out_specs=vmem,
        scratch_shapes=[
            pltpu.VMEM((blocks, frames, width), jnp.bfloat16),
            pltpu.VMEM((blocks, frames, 128), F32),
            pltpu.VMEM((total, frames, width), jnp.bfloat16),
            pltpu.VMEM((frames, width), jnp.bfloat16),
            pltpu.VMEM((frames, width), jnp.bfloat16),
            pltpu.VMEM((blocks, frames, 2 * width), F32),
            pltpu.VMEM((total, frames // SPAN, frames, SPAN), jnp.bfloat16),
            pltpu.SMEM((5, total), jnp.int32),
            pltpu.SemaphoreType.DMA((total,)),
            pltpu.SemaphoreType.DMA((total,)),
            pltpu.SemaphoreType.DMA,
            pltpu.SemaphoreType.DMA,
        ],
        compiler_params=pltpu.CompilerParams(vmem_limit_bytes=60 * 1024 * 1024),
        name="second_pass",
    )(*tables, ok, student, every, begun, kept, rows, far, own)


def exchange_kernel(n_dp, n_tm, valid_ref, ask_ref, side_ref, send_ref, own_ref, sum_ref, far_ref, lse_ref, loss_ref,
                    inc, reply, across, ask_buf, s1, r1, s2, r2, s3, r3, ask_sem):
    me, tm = lax.axis_index("dp"), lax.axis_index("tm")
    asks = pltpu.make_async_copy(ask_ref, ask_buf, ask_sem)
    asks.start()
    others = [(me + o) % n_dp for o in range(1, n_dp)]
    beside = [(tm + o) % n_tm for o in range(1, n_tm)]
    barrier = pltpu.get_barrier_semaphore()
    for to in others:
        pl.semaphore_signal(barrier, inc=1, device_id=(to, tm), device_id_type=MESH)
    for to in beside:
        pl.semaphore_signal(barrier, inc=1, device_id=(me, to), device_id_type=MESH)
    inc[me] = send_ref[me]
    pl.semaphore_wait(barrier, n_dp - 1 + n_tm - 1)

    def ship(src, dst, sent, got, where):
        pltpu.make_async_remote_copy(
            src_ref=src, dst_ref=dst, send_sem=sent, recv_sem=got, device_id=where, device_id_type=MESH).start()

    for to in others:
        ship(send_ref.at[to], inc.at[me], s1, r1, (to, tm))
    settle(inc, r1, n_dp - 1)
    asks.wait()
    terms = sum_ref[...] + side_ref[0]
    frame = lax.broadcasted_iota(jnp.int32, (8, 128), 0) * 128 + lax.broadcasted_iota(jnp.int32, (8, 128), 1)
    for a in range(2):
        best = own_ref[a]
        for p in range(n_dp):
            best = jnp.maximum(best, inc[p] + ask_buf[p, a])
        total = jnp.exp(own_ref[a] - best)
        for p in range(n_dp):
            total = total + jnp.exp(inc[p] + ask_buf[p, a] - best)
        lse = jnp.where(frame < valid_ref[(me * n_tm + tm) * 2 + a], best + jnp.log(total), 0.0)
        lse_ref[a] = lse
        terms = terms + lse
    terms = jnp.sum(terms, axis=0, keepdims=True)
    for p in range(n_dp):
        share = ask_buf[p, 2]
        reply[p, :8, :] = lse_ref[0] * (1.0 - share) + lse_ref[1] * share
        reply[p, 8:9, :] = terms
    far_ref[me] = reply[me]
    sent = pl.ds(0, 9)
    for to in others:
        ship(reply.at[to, sent], far_ref.at[me, sent], s2, r2, (to, tm))
    settle(far_ref.at[:, sent], r2, n_dp - 1)
    rows = far_ref[0, 8:9, :]
    for p in range(1, n_dp):
        rows = rows + far_ref[p, 8:9, :]
    across[tm] = jnp.broadcast_to(rows, (8, 128))
    for to in beside:
        ship(across.at[tm], across.at[tm], s3, r3, (me, to))
    settle(across, r3, n_tm - 1)
    rows = across[0]
    for t in range(1, n_tm):
        rows = rows + across[t]
    loss_ref[0] = jnp.sum(rows[0:1] * side_ref[1, 0:1, :])
    settle(send_ref, s1, n_dp - 1)
    settle(reply.at[:, sent], s2, n_dp - 1)
    settle(across, s3, n_tm - 1)


def exchange(valid, ask, side, send, own, sums, n_tm):
    n_dp = send.shape[0]
    smem, vmem = pl.BlockSpec(memory_space=pltpu.SMEM), pl.BlockSpec(memory_space=pltpu.VMEM)
    return pl.pallas_call(
        functools.partial(exchange_kernel, n_dp, n_tm),
        out_shape=(
            jax.ShapeDtypeStruct((n_dp, 16, 128), F32),
            jax.ShapeDtypeStruct((2, 8, 128), F32),
            jax.ShapeDtypeStruct((1,), F32),
        ),
        in_specs=[smem, pl.BlockSpec(memory_space=pl.ANY)] + [vmem] * 4,
        out_specs=(vmem, vmem, smem),
        scratch_shapes=[
            pltpu.VMEM((n_dp, 8, 128), F32), pltpu.VMEM((n_dp, 16, 128), F32),
            pltpu.VMEM((n_tm, 8, 128), F32), pltpu.VMEM(ask.shape, F32),
        ] + [pltpu.SemaphoreType.DMA] * 7,
        compiler_params=pltpu.CompilerParams(collective_id=1, has_side_effects=True),
        name="exchange",
    )(valid, ask, side, send, own, sums)


def body(student, teacher, partner_dp, partner_slot, valid_frames):
    n_dp, n_tm = lax.axis_size("dp"), lax.axis_size("tm")
    blocks, frames, width = student.shape
    tiles = partner_dp.shape[1] + 1
    tables = (partner_dp.T, partner_slot.T, valid_frames)
    every, begun, sofar, ask, side, order, cols = gather(teacher, student, tables, n_dp, n_tm)
    every = every.reshape(n_dp * blocks, frames, width)
    tables = tables + (order,)
    rows, send, own, ok, sums, kept = first_pass(tables, student, every, sofar, cols, n_dp, n_tm, tiles)
    far, lse, loss = exchange(valid_frames, ask, side, send, own, sums, n_tm)
    grad = second_pass(tables, ok, student, every, begun, kept, rows, far, lse, n_tm, tiles)
    return (loss[0], grad)


def solution(mesh):
    placed = (P(("dp", "tm"), None, None), P(("dp", "tm"), None, None), P(), P(), P())
    return jax.shard_map(
        body,
        mesh=mesh,
        in_specs=placed,
        out_specs=(P(), P(("dp", "tm"), None, None)),
        check_vma=False,
    )
```
